32 devices in a mesh: slide: 2 (over x), row: 16 (over z, y, core).
Axes of the slice: x: 2, y: 2, z: 4, core: 2. Of those that a mesh axis runs over, the one named last changes fastest.
Arguments:
- query_states: bfloat16 [32, 1, 4, 64, 768], P(('slide', 'row')), parts along dimension 0, may hold values from -240 to 240
- key_states: bfloat16 [32, 1, 4, 64, 768], P(('slide', 'row')), parts along dimension 0, may hold values from -6 to 6
- value_states: bfloat16 [32, 1, 4, 64, 768], P(('slide', 'row')), parts along dimension 0, may hold values from -6 to 6
- grad_output: bfloat16 [32, 1, 4, 64, 768], P(('slide', 'row')), parts along dimension 0, may hold values from -6 to 6
- tissue_map: int32 [4, 32], P('slide'), parts along dimension 0, may hold values from 0 to 1, as said below
Outputs:
- attended: bfloat16 [32, 1, 4, 64, 768], P(('slide', 'row')), parts along dimension 0
- grad_query: bfloat16 [32, 1, 4, 64, 768], P(('slide', 'row')), parts along dimension 0
- grad_key: bfloat16 [32, 1, 4, 64, 768], P(('slide', 'row')), parts along dimension 0
- grad_value: bfloat16 [32, 1, 4, 64, 768], P(('slide', 'row')), parts along dimension 0
The draws below stay inside these ranges and needn't reach their ends.
There are 2 independent parts, one for each index of `slide`. The reference program is written for one: setup_inputs(seed, part) draws one part's arguments, and reference() takes and returns one part's arrays. A program takes and returns all parts, laid end to end along the dimension named above; each array names one. Nothing has to cross between parts.
Inputs may be any that keep to these rules, and one draw needn't show every extreme that they name: `tissue_map`: 1 marks a tile that holds tissue; every tile of tile row 1 holds tissue.
All inputs are finite; a program needn't handle non-finite values.
Results may differ from the reference program's by a relative error of at most 0.023.
Values may be sent and summed in bfloat16 or wider, within the bound.
A program may use at most 128 MiB of HBM per device.

```python
import jax
import jax.numpy as jnp
from jax import lax

HEADS = 12
HEAD_DIM = 64
TILE_SIDE = 8
WINDOW = 13
GRID_C = 8
TILE_ROWS = 1
TILE_COLS = 4
BLOCKS = 16
ROWS_ALL = 2
COLS_ALL = 32
PIXELS = 64
INNER = 768


def paired_keys(key):
    full_shape = (BLOCKS, TILE_ROWS, TILE_COLS, TILE_SIDE * TILE_SIDE, HEADS * HEAD_DIM)
    drawn_keys = jnp.clip(jax.random.normal(jax.random.fold_in(key, 11), full_shape, jnp.float32), -6.0, 6.0)
    return drawn_keys


def draw_key_states(key, part):
    drawn_keys = paired_keys(key)
    return drawn_keys.astype(jnp.bfloat16)


def draw_query_states(key, part):
    drawn_keys = paired_keys(key)
    full_shape = drawn_keys.shape
    queries = jnp.clip(jax.random.normal(jax.random.fold_in(key, 13), full_shape, jnp.float32), -6.0, 6.0)
    return queries.astype(jnp.bfloat16)


def draw_tissue_map(key, part):
    density = jax.random.randint(jax.random.fold_in(key, 21), (ROWS_ALL, 1), 10, 101)
    chance = jax.random.randint(jax.random.fold_in(key, 22), (ROWS_ALL, COLS_ALL), 0, 100)
    band = jnp.arange(ROWS_ALL, dtype=jnp.int32)[:, None] == ROWS_ALL // 2
    return ((chance < density) | band).astype(jnp.int32)


def block_levels(key, shape, split, low, high):
    level, own = 1.0, jax.random.fold_in(key, 6)
    for position, blocks in split:
        steps = jnp.exp(jax.random.uniform(jax.random.fold_in(own, position), (blocks,), jnp.float32, low / len(split), high / len(split)))
        level = level * jnp.repeat(steps, shape[position] // blocks).reshape([-1 if axis == position else 1 for axis in range(len(shape))])
    return level


def noise(own_key, extent, spread, bound, cuts=(), kind=jnp.bfloat16):
    loudness = block_levels(own_key, extent, cuts, -0.22, 0.18) if cuts else 1.0
    array = jax.random.normal(own_key, extent, jnp.float32) * spread * loudness
    return jnp.minimum(jnp.maximum(array, -bound), bound).astype(kind)


def setup_inputs(seed: int = 0, part: int = 0) -> dict:
    key_of = jax.random.split(jax.random.key(seed), 6)
    own_keys = jax.random.split(jax.random.fold_in(key_of[5], part), 6)
    query_states = draw_query_states(jax.random.fold_in(jax.random.fold_in(key_of[5], part), 71), part)
    key_states = draw_key_states(jax.random.fold_in(jax.random.fold_in(key_of[5], part), 71), part)
    value_states = noise(own_keys[2], (BLOCKS, TILE_ROWS, TILE_COLS, PIXELS, INNER), 1.0, 6.0, ((0, 16),))
    grad_output = noise(own_keys[3], (BLOCKS, TILE_ROWS, TILE_COLS, PIXELS, INNER), 1.0, 6.0, ((0, 16),))
    tissue_map = draw_tissue_map(jax.random.fold_in(jax.random.fold_in(key_of[5], part), 71), part)
    return dict(query_states=query_states, key_states=key_states, value_states=value_states, grad_output=grad_output, tissue_map=tissue_map)


MASKED_SCORE = -1e30


def window_table():
    half_window = (WINDOW - 1) // 2
    pixel_index = jnp.arange(TILE_SIDE * TILE_SIDE, dtype=jnp.int32)
    pix_row = pixel_index // TILE_SIDE
    pix_col = pixel_index % TILE_SIDE
    tables = []
    for row_step in (-1, 0, 1):
        for col_step in (-1, 0, 1):
            row_gap = TILE_SIDE * row_step + pix_row[None, :] - pix_row[:, None]
            col_gap = TILE_SIDE * col_step + pix_col[None, :] - pix_col[:, None]
            tables.append((jnp.abs(row_gap) <= half_window) & (jnp.abs(col_gap) <= half_window))
    return jnp.stack(tables)


def widen_to(operand, widen):
    if widen:
        return operand.astype(jnp.float32)
    return operand


def to_grid(operand):
    operand = jnp.roll(operand, GRID_C // 2, axis=0)
    block_count, tile_rows, tile_cols, pixel_count, inner_width = operand.shape
    grid_rows = block_count // GRID_C
    moved = operand.reshape(grid_rows, GRID_C, tile_rows, tile_cols, pixel_count, inner_width).transpose(0, 2, 1, 3, 4, 5)
    return moved.reshape(grid_rows * tile_rows, GRID_C * tile_cols, pixel_count, inner_width)


def to_blocks(operand):
    rows_all, cols_all, pixel_count, inner_width = operand.shape
    moved = operand.reshape(rows_all // TILE_ROWS, TILE_ROWS, GRID_C, TILE_COLS, pixel_count, inner_width).transpose(0, 2, 1, 3, 4, 5)
    moved = moved.reshape(-1, TILE_ROWS, TILE_COLS, pixel_count, inner_width)
    return jnp.roll(moved, -(GRID_C // 2), axis=0)


def attend_tiles(query4, grad4, key4, value4, allowed, tissue_rows, widen):
    score_scale = HEAD_DIM ** -0.5
    usable = allowed[:, None]
    scores = jnp.einsum("cqhe,ckhe->chqk", widen_to(query4, widen), widen_to(key4, widen), preferred_element_type=jnp.float32) * score_scale
    masked = jnp.where(usable, scores, MASKED_SCORE)
    row_peak = jnp.max(masked, axis=-1, keepdims=True)
    row_total = jnp.sum(jnp.exp(masked - row_peak), axis=-1, keepdims=True)
    log_total = row_peak + jnp.log(row_total)
    weights_full = jnp.where(usable, jnp.exp(scores - log_total), 0.0)
    weights_low = weights_full.astype(jnp.bfloat16)
    mixture = jnp.einsum("chqk,ckhe->cqhe", widen_to(weights_low, widen), widen_to(value4, widen), preferred_element_type=jnp.float32)
    attended = (mixture * tissue_rows[:, None, None, None]).astype(jnp.bfloat16)
    out_dot = jnp.einsum("cqhe,cqhe->chq", widen_to(attended, widen), widen_to(grad4, widen), preferred_element_type=jnp.float32)
    grad_probe = jnp.einsum("cqhe,ckhe->chqk", widen_to(grad4, widen), widen_to(value4, widen), preferred_element_type=jnp.float32)
    grad_score = (weights_full * (grad_probe - out_dot[..., None])).astype(jnp.bfloat16)
    grad_query = (jnp.einsum("chqk,ckhe->cqhe", widen_to(grad_score, widen), widen_to(key4, widen), preferred_element_type=jnp.float32) * score_scale).astype(jnp.bfloat16)
    grad_key = jnp.einsum("chqk,cqhe->ckhe", widen_to(grad_score, widen), widen_to(query4, widen), preferred_element_type=jnp.float32) * score_scale
    grad_value = jnp.einsum("chqk,cqhe->ckhe", widen_to(weights_low, widen), widen_to(grad4, widen), preferred_element_type=jnp.float32)
    return attended, grad_query, log_total[..., 0], out_dot, grad_key, grad_value


def key_terms(query4, grad4, key4, value4, allowed, log_total, out_dot, widen):
    score_scale = HEAD_DIM ** -0.5
    usable = allowed[:, None]
    scores = jnp.einsum("cqhe,ckhe->chqk", widen_to(query4, widen), widen_to(key4, widen), preferred_element_type=jnp.float32) * score_scale
    weights_full = jnp.where(usable, jnp.exp(scores - log_total[..., None]), 0.0)
    weights_low = weights_full.astype(jnp.bfloat16)
    grad_probe = jnp.einsum("cqhe,ckhe->chqk", widen_to(grad4, widen), widen_to(value4, widen), preferred_element_type=jnp.float32)
    grad_score = (weights_full * (grad_probe - out_dot[..., None])).astype(jnp.bfloat16)
    grad_key = jnp.einsum("chqk,cqhe->ckhe", widen_to(grad_score, widen), widen_to(query4, widen), preferred_element_type=jnp.float32) * score_scale
    grad_value = jnp.einsum("chqk,cqhe->ckhe", widen_to(weights_low, widen), widen_to(grad4, widen), preferred_element_type=jnp.float32)
    return grad_key, grad_value


def reference(query_states, key_states, value_states, grad_output, tissue_map):
    query_states = to_grid(query_states)
    key_states = to_grid(key_states)
    value_states = to_grid(value_states)
    grad_output = to_grid(grad_output)
    rows_all, column_total = tissue_map.shape
    pixel_count = TILE_SIDE * TILE_SIDE
    window_masks = window_table()
    tissue = tissue_map.astype(jnp.float32)
    grad_eff = (grad_output * tissue[:, :, None, None]).astype(jnp.bfloat16)

    def framed(operand):
        return jnp.pad(operand, ((1, 1), (1, 1), (0, 0), (0, 0)))

    key_pad = framed(key_states)
    value_pad = framed(value_states)
    tissue_pad = jnp.pad(tissue_map, ((1, 1), (1, 1)))

    def query_row(row_index):
        key_tiles, value_tiles, flag_tiles = [], [], []
        for row_step in (-1, 0, 1):
            where_row = row_index + 1 + row_step
            key_band = lax.dynamic_index_in_dim(key_pad, where_row, 0, keepdims=False)
            value_strip = lax.dynamic_index_in_dim(value_pad, where_row, 0, keepdims=False)
            flag_band = lax.dynamic_index_in_dim(tissue_pad, where_row, 0, keepdims=False)
            for col_step in (-1, 0, 1):
                key_tiles.append(key_band[1 + col_step:1 + col_step + column_total])
                value_tiles.append(value_strip[1 + col_step:1 + col_step + column_total])
                flag_tiles.append(flag_band[1 + col_step:1 + col_step + column_total])
        key4 = jnp.stack(key_tiles, 1).reshape(column_total, 9 * pixel_count, HEADS, HEAD_DIM)
        value4 = jnp.stack(value_tiles, 1).reshape(column_total, 9 * pixel_count, HEADS, HEAD_DIM)
        flags = jnp.stack(flag_tiles, 1)
        allowed = (window_masks.transpose(1, 0, 2)[None] & (flags[:, None, :, None] > 0)).reshape(column_total, pixel_count, 9 * pixel_count)
        query4 = lax.dynamic_index_in_dim(query_states, row_index, 0, keepdims=False).reshape(column_total, pixel_count, HEADS, HEAD_DIM)
        grad4 = lax.dynamic_index_in_dim(grad_eff, row_index, 0, keepdims=False).reshape(column_total, pixel_count, HEADS, HEAD_DIM)
        tissue_rows = lax.dynamic_index_in_dim(tissue, row_index, 0, keepdims=False)
        attended, grad_query, log_total, out_dot, unused_key, unused_value = attend_tiles(query4, grad4, key4, value4, allowed, tissue_rows, True)
        return attended.reshape(column_total, pixel_count, INNER), grad_query.reshape(column_total, pixel_count, INNER), log_total, out_dot

    row_ids = jnp.arange(rows_all, dtype=jnp.int32)
    attended, grad_query, log_total, out_dot = lax.map(query_row, row_ids)

    query_pad = framed(query_states)
    gradient_padded = framed(grad_eff)
    log_pad = framed(log_total)
    dot_pad = framed(out_dot)

    def key_row(row_index):
        query_tiles, grad_tiles, log_tiles, dot_tiles = [], [], [], []
        for row_step in (-1, 0, 1):
            where_row = row_index + 1 - row_step
            query_band = lax.dynamic_index_in_dim(query_pad, where_row, 0, keepdims=False)
            grad_band = lax.dynamic_index_in_dim(gradient_padded, where_row, 0, keepdims=False)
            log_band = lax.dynamic_index_in_dim(log_pad, where_row, 0, keepdims=False)
            dot_band = lax.dynamic_index_in_dim(dot_pad, where_row, 0, keepdims=False)
            for col_step in (-1, 0, 1):
                query_tiles.append(query_band[1 - col_step:1 - col_step + column_total])
                grad_tiles.append(grad_band[1 - col_step:1 - col_step + column_total])
                log_tiles.append(log_band[1 - col_step:1 - col_step + column_total])
                dot_tiles.append(dot_band[1 - col_step:1 - col_step + column_total])
        query4 = jnp.stack(query_tiles, 1).reshape(column_total, 9 * pixel_count, HEADS, HEAD_DIM)
        grad4 = jnp.stack(grad_tiles, 1).reshape(column_total, 9 * pixel_count, HEADS, HEAD_DIM)
        log4 = jnp.stack(log_tiles, 2).reshape(column_total, HEADS, 9 * pixel_count)
        dot4 = jnp.stack(dot_tiles, 2).reshape(column_total, HEADS, 9 * pixel_count)
        key4 = lax.dynamic_index_in_dim(key_states, row_index, 0, keepdims=False).reshape(column_total, pixel_count, HEADS, HEAD_DIM)
        value4 = lax.dynamic_index_in_dim(value_states, row_index, 0, keepdims=False).reshape(column_total, pixel_count, HEADS, HEAD_DIM)
        flags = lax.dynamic_index_in_dim(tissue_map, row_index, 0, keepdims=False)
        allowed = (window_masks[None] & (flags[:, None, None, None] > 0)).reshape(column_total, 9 * pixel_count, pixel_count)
        grad_key, grad_value = key_terms(query4, grad4, key4, value4, allowed, log4, dot4, True)
        return grad_key.astype(jnp.bfloat16).reshape(column_total, pixel_count, INNER), grad_value.astype(jnp.bfloat16).reshape(column_total, pixel_count, INNER)

    grad_key, grad_value = lax.map(key_row, row_ids)
    return (to_blocks(attended), to_blocks(grad_query), to_blocks(grad_key), to_blocks(grad_value))
```

```python
import functools

import jax
import jax.numpy as jnp
from jax import lax
from jax.experimental import pallas as pl
from jax.experimental.pallas import tpu as pltpu
from jax.sharding import PartitionSpec as P

HEAD_DIM = 64
TILE_SIDE = 8
WINDOW = 13
GRID_C = 8
PIX = TILE_SIDE * TILE_SIDE
HALF = (WINDOW - 1) // 2
REACH = HALF * TILE_SIDE
SKIP = PIX - REACH
WIDTH = 256
SUB = WIDTH // HEAD_DIM
MASKED = -1e30
F32 = jnp.float32
BF16 = jnp.bfloat16
MESH = pl.DeviceIdType.MESH


def dot(a, b, ca, cb):
    return lax.dot_general(a, b, (((ca,), (cb,)), ((), ())), preferred_element_type=F32)


def fold_rows(x):
    total = x[:PIX]
    for i in range(1, SUB):
        total = total + x[i * PIX : (i + 1) * PIX]
    return total


def kernel(
    count, nv, cols, groups,
    tissue, q_ref, k_ref, v_ref, g_ref, att_ref, dq_ref, dk_ref, dv_ref,
    q_s, g_s, rowx, vertx, bias, drow, dvert, hrow_s, hvert_s, hrow_r, hvert_r, vert_s, vert_r, outs,
    load_sem, store_sem, side_ss, side_rs, up_ss, up_rs, edge_ss, edge_rs,
    hrow_ss, hrow_rs, hvert_ss, hvert_rs, vert_ss, vert_rs,
):
    slide, me = lax.axis_index("slide"), lax.axis_index("row")
    block = lax.rem(me + GRID_C // 2, count)
    grid_row, grid_col = lax.div(block, GRID_C), lax.rem(block, GRID_C)
    block_rows = count // GRID_C

    def at(distance):
        return (slide, lax.rem(me + distance + count, count))

    left, right = at(-1), at(1)
    if nv == 1:
        above = grid_row == 1
        distance = [GRID_C]
        start = [jnp.where(above, 0, SKIP)]
        places = [(jnp.where(above, -1, 1), jnp.where(above, -HALF, TILE_SIDE))]
        seam_left = grid_col == GRID_C // 2
        seam_right = grid_col == GRID_C // 2 - 1
        seam = jnp.logical_or(seam_left, seam_right)
        across = at(jnp.where(seam_left, GRID_C - 1, GRID_C + 1))
    else:
        distance = [GRID_C, -GRID_C]
        start = [jnp.int32(SKIP), jnp.int32(0)]
        places = [(-1, -HALF), (1, TILE_SIDE)]
        seam_left = seam_right = seam = None
    start = [pl.multiple_of(x, 16) for x in start]
    seams = (seam_left, seam_right)

    def lanes(i):
        return pl.ds(pl.multiple_of(i * WIDTH, WIDTH), WIDTH)

    kv = (k_ref, v_ref)
    loads = [pltpu.make_async_copy(x, y, load_sem.at[j]) for j, (x, y) in enumerate((
        (k_ref, rowx.at[0, pl.ds(1, cols)]), (v_ref, rowx.at[1, pl.ds(1, cols)]), (q_ref, q_s), (g_ref, g_s),
    ))]

    def remote(src, dst, ss, rs, device):
        return pltpu.make_async_remote_copy(
            src_ref=src, dst_ref=dst, send_sem=ss, recv_sem=rs, device_id=device, device_id_type=MESH
        )

    def up(i, z, v):
        return remote(
            kv[z].at[:, pl.ds(start[v], REACH), lanes(i)],
            vertx.at[z, v, pl.ds(1, cols), :, lanes(i)],
            up_ss.at[i, z, v], up_rs.at[i, z, v], at(distance[v]),
        )

    def sideways(z, d):
        return remote(
            kv[z].at[0 if d == 0 else cols - 1], rowx.at[z, cols + 1 if d == 0 else 0],
            side_ss.at[z, d], side_rs.at[z, d], left if d == 0 else right,
        )

    def edge(i, z, d):
        return remote(
            vertx.at[z, :, 1 if d == 0 else cols, :, lanes(i)], vertx.at[z, :, cols + 1 if d == 0 else 0, :, lanes(i)],
            edge_ss.at[i, z, d], edge_rs.at[i, z, d], left if d == 0 else right,
        )

    def diagonal(i, z, d):
        return remote(
            kv[z].at[0 if d == 0 else cols - 1, pl.ds(start[0], REACH), lanes(i)],
            vertx.at[z, 0, cols + 1 if d == 0 else 0, :, lanes(i)],
            edge_ss.at[i, z, d], edge_rs.at[i, z, d], across,
        )

    def row_back(i, d):
        return remote(
            hrow_s.at[d, :, :, lanes(i)], hrow_r.at[1 - d, :, :, lanes(i)],
            hrow_ss.at[i, d], hrow_rs.at[i, d], left if d == 0 else right,
        )

    def vert_back(i, d):
        device = left if d == 0 else right
        if seam is not None:
            device = (slide, jnp.where(seams[d], across[1], device[1]))
        return remote(
            hvert_s.at[d, :, :, :, lanes(i)], hvert_r.at[1 - d, :, :, :, lanes(i)],
            hvert_ss.at[i, d], hvert_rs.at[i, d], device,
        )

    def down(i, v):
        return remote(
            vert_s.at[:, v, :, :, lanes(i)], vert_r.at[:, v, :, :, lanes(i)],
            vert_ss.at[i, v], vert_rs.at[i, v], at(-distance[v]),
        )

    def store(i, j):
        return pltpu.make_async_copy(
            outs.at[j, :, :, lanes(i)], (att_ref, dq_ref, dk_ref, dv_ref)[j].at[:, :, lanes(i)], store_sem.at[i, j]
        )

    barrier = pltpu.get_barrier_semaphore()
    for device in [left, right] + [at(x) for x in distance]:
        pl.semaphore_signal(barrier, inc=1, device_id=device, device_id_type=MESH)
    if seam is not None:
        @pl.when(seam)
        def _():
            pl.semaphore_signal(barrier, inc=1, device_id=across, device_id_type=MESH)
    for copy in loads:
        copy.start()
    pl.semaphore_wait(barrier, 2 + nv + (0 if seam is None else seam.astype(jnp.int32)))

    for z in range(2):
        for v in range(nv):
            up(0, z, v).start()
    for z in range(2):
        for d in range(2):
            sideways(z, d).start()
    for i in range(1, groups):
        for z in range(2):
            for v in range(nv):
                up(i, z, v).start()
    if seam is not None:
        for d in range(2):
            @pl.when(seams[d])
            def _():
                for i in range(groups):
                    for z in range(2):
                        diagonal(i, z, d).start()

    query = lax.broadcasted_iota(jnp.int32, (PIX, WIDTH), 1) % PIX
    line = lax.broadcasted_iota(jnp.int32, (PIX, WIDTH), 0)
    top = 0
    for step_row, first, rows in [(0, 0, PIX)] + [(r, f, REACH) for r, f in places]:
        row_gap = first + line[:rows] // TILE_SIDE - query[:rows] // TILE_SIDE
        row = grid_row + step_row
        for step in (-1, 0, 1):
            col_gap = TILE_SIDE * step + line[:rows] % TILE_SIDE - query[:rows] % TILE_SIDE
            near = (jnp.abs(row_gap) <= HALF) & (jnp.abs(col_gap) <= HALF)
            near = jnp.where(near, 0.0, MASKED)
            for c in range(cols):
                col = grid_col * cols + c + step
                inside = (row >= 0) & (row < block_rows) & (col >= 0) & (col < GRID_C * cols)
                flag = tissue[jnp.clip(row, 0, block_rows - 1), jnp.clip(col, 0, GRID_C * cols - 1)]
                shut = jnp.where(inside & (flag > 0), 0.0, MASKED)
                bias[c, top : top + rows] = jnp.minimum(near, shut)
            top += rows
    drow[...] = jnp.zeros_like(drow)
    dvert[...] = jnp.zeros_like(dvert)

    same = (
        lax.broadcasted_iota(jnp.int32, (WIDTH, WIDTH), 0) // PIX
        == lax.broadcasted_iota(jnp.int32, (WIDTH, WIDTH), 1) // HEAD_DIM
    )
    same_low = jnp.where(same, 1.0, 0.0).astype(BF16)

    def keys_of(z, c, i):
        parts = [rowx[z, c : c + 3, :, lanes(i)].reshape(3 * PIX, WIDTH)]
        for v in range(nv):
            parts.append(vertx[z, v, c : c + 3, :, lanes(i)].reshape(3 * REACH, WIDTH))
        return jnp.concatenate(parts, axis=0)

    def attend(i):
        for c in range(cols):
            flag = tissue[grid_row, grid_col * cols + c].astype(F32)
            live = jnp.where(same, flag, 0.0)
            q = q_s[c, :, lanes(i)] * 0.125
            qbd = jnp.concatenate([q] * SUB, axis=0) * same_low
            g = g_s[c, :, lanes(i)]
            gbd = jnp.concatenate([g] * SUB, axis=0) * live.astype(BF16)
            kc, vc = keys_of(0, c, i), keys_of(1, c, i)
            s = dot(kc, qbd, 1, 1) + bias[c]
            peak = jnp.max(s, axis=0, keepdims=True)
            p = jnp.exp(s - peak)
            w = p * (1.0 / jnp.sum(p, axis=0, keepdims=True))
            w_low = w.astype(BF16)
            att_t = (dot(vc, w_low, 0, 0) * live).astype(BF16)
            outs[0, c, :, lanes(i)] = fold_rows(att_t.T)
            out_dot = jnp.sum(att_t.astype(F32) * gbd.T.astype(F32), axis=0, keepdims=True)
            probe = dot(vc, gbd, 1, 1)
            ds = (w * (probe - out_dot)).astype(BF16)
            dq = jnp.where(same, dot(ds, kc, 0, 0), 0.0)
            outs[1, c, :, lanes(i)] = (fold_rows(dq) * 0.125).astype(BF16)
            for z, term in enumerate((dot(ds, qbd, 1, 0), dot(w_low, gbd, 1, 0))):
                drow[z, c : c + 3, :, lanes(i)] += term[: 3 * PIX].reshape(3, PIX, WIDTH)
                for v in range(nv):
                    first = 3 * (PIX + v * REACH)
                    dvert[z, v, c : c + 3, :, lanes(i)] += term[first : first + 3 * REACH].reshape(3, REACH, WIDTH)

    def merge(i):
        for d in range(2):
            row_back(i, d).wait_recv()
            vert_back(i, d).wait_recv()
        for z in range(2):
            for v in range(nv):
                for c in range(cols):
                    vert_s[z, v, c, :, lanes(i)] = dvert[z, v, c + 1, :, lanes(i)].astype(BF16)
        for d, c in ((0, 0), (1, cols - 1)):
            def add(d=d, c=c):
                for z in range(2):
                    for v in range(nv):
                        vert_s[z, v, c, :, lanes(i)] = (
                            dvert[z, v, c + 1, :, lanes(i)] + hvert_r[d, z, v, :, lanes(i)].astype(F32)
                        ).astype(BF16)
            if seam is None:
                add()
            else:
                pl.when(jnp.logical_not(seams[d]))(add)
        for v in range(nv):
            down(i, v).start()

    def step(i, _):
        for z in range(2):
            for v in range(nv):
                up(i, z, v).wait_recv()
        for d in range(2):
            def forward(d=d):
                for z in range(2):
                    edge(i, z, d).start()
            if seam is None:
                forward()
            else:
                pl.when(jnp.logical_not(seams[d]))(forward)

        @pl.when(i > 0)
        def _():
            merge(i - 1)

        @pl.when(i == 0)
        def _():
            for copy in loads:
                copy.wait()
            for z in range(2):
                for d in range(2):
                    sideways(z, d).wait_recv()

        for z in range(2):
            for d in range(2):
                edge(i, z, d).wait_recv()
        attend(i)
        for d, tile in ((0, 0), (1, cols + 1)):
            for z in range(2):
                hrow_s[d, z, :, lanes(i)] = drow[z, tile, :, lanes(i)].astype(BF16)
                for v in range(nv):
                    hvert_s[d, z, v, :, lanes(i)] = dvert[z, v, tile, :, lanes(i)].astype(BF16)
            row_back(i, d).start()
            vert_back(i, d).start()
        for j in range(2):
            store(i, j).start()
        return 0

    lax.fori_loop(0, groups, step, 0)
    merge(groups - 1)

    def finish(i, _):
        for v in range(nv):
            down(i, v).wait_recv()
        for z in range(2):
            drow[z, 1, :, lanes(i)] += hrow_r[0, z, :, lanes(i)].astype(F32)
            drow[z, cols, :, lanes(i)] += hrow_r[1, z, :, lanes(i)].astype(F32)
            for v in range(nv):
                for c in range(cols):
                    drow[z, c + 1, pl.ds(start[v], REACH), lanes(i)] += vert_r[z, v, c, :, lanes(i)].astype(F32)
            if seam is not None:
                for d, c in ((0, 0), (1, cols - 1)):
                    @pl.when(seams[d])
                    def _():
                        drow[z, c + 1, pl.ds(start[0], REACH), lanes(i)] += hvert_r[d, z, 0, :, lanes(i)].astype(F32)
            outs[2 + z, :, :, lanes(i)] = drow[z, 1 : cols + 1, :, lanes(i)].astype(BF16)
            store(i, 2 + z).start()
        return 0

    lax.fori_loop(0, groups, finish, 0)

    def drain(i, _):
        for z in range(2):
            for v in range(nv):
                up(i, z, v).wait_send()
            for d in range(2):
                edge(i, z, d).wait_send()
        for d in range(2):
            row_back(i, d).wait_send()
            vert_back(i, d).wait_send()
        for v in range(nv):
            down(i, v).wait_send()
        for j in range(4):
            store(i, j).wait()
        return 0

    for z in range(2):
        for d in range(2):
            sideways(z, d).wait_send()
    lax.fori_loop(0, groups, drain, 0)


def local(query_states, key_states, value_states, grad_output, tissue_map):
    shape = query_states.shape
    cols, inner = shape[2], shape[4]
    q, k, v, g = (x.reshape(cols, PIX, inner) for x in (query_states, key_states, value_states, grad_output))
    count = lax.axis_size("row")
    nv = 1 if count // GRID_C == 2 else 2
    groups = inner // WIDTH
    seen = 3 * (PIX + nv * REACH)
    dma = pltpu.SemaphoreType.DMA
    anywhere = pl.BlockSpec(memory_space=pl.ANY)
    out = pl.pallas_call(
        functools.partial(kernel, count, nv, cols, groups),
        in_specs=[pl.BlockSpec(memory_space=pltpu.SMEM)] + [anywhere] * 4,
        out_specs=[anywhere] * 4,
        out_shape=[jax.ShapeDtypeStruct((cols, PIX, inner), BF16)] * 4,
        scratch_shapes=[
            pltpu.VMEM((cols, PIX, inner), BF16),
            pltpu.VMEM((cols, PIX, inner), BF16),
            pltpu.VMEM((2, cols + 2, PIX, inner), BF16),
            pltpu.VMEM((2, nv, cols + 2, REACH, inner), BF16),
            pltpu.VMEM((cols, seen, WIDTH), F32),
            pltpu.VMEM((2, cols + 2, PIX, inner), F32),
            pltpu.VMEM((2, nv, cols + 2, REACH, inner), F32),
            pltpu.VMEM((2, 2, PIX, inner), BF16),
            pltpu.VMEM((2, 2, nv, REACH, inner), BF16),
            pltpu.VMEM((2, 2, PIX, inner), BF16),
            pltpu.VMEM((2, 2, nv, REACH, inner), BF16),
            pltpu.VMEM((2, nv, cols, REACH, inner), BF16),
            pltpu.VMEM((2, nv, cols, REACH, inner), BF16),
            pltpu.VMEM((4, cols, PIX, inner), BF16),
            dma((4,)), dma((groups, 4)),
            dma((2, 2)), dma((2, 2)),
            dma((groups, 2, nv)), dma((groups, 2, nv)),
            dma((groups, 2, 2)), dma((groups, 2, 2)),
            dma((groups, 2)), dma((groups, 2)),
            dma((groups, 2)), dma((groups, 2)),
            dma((groups, nv)), dma((groups, nv)),
        ],
        compiler_params=pltpu.CompilerParams(
            collective_id=0, has_side_effects=True, vmem_limit_bytes=40 << 20
        ),
        cost_estimate=pl.CostEstimate(
            flops=groups * cols * seen * WIDTH * WIDTH * 2 * 6,
            bytes_accessed=8 << 20,
            transcendentals=groups * cols * seen * WIDTH,
        ),
    )(tissue_map, q, k, v, g)
    return tuple(x.reshape(shape) for x in out)


def solution(mesh):
    blocks = P(("slide", "row"), None, None, None, None)
    return jax.shard_map(
        local,
        mesh=mesh,
        in_specs=(blocks, blocks, blocks, blocks, P("slide", None)),
        out_specs=(blocks, blocks, blocks, blocks),
        check_vma=False,
    )
```

```python
import functools

import jax
import jax.numpy as jnp
from jax import lax
from jax.experimental import pallas as pl
from jax.experimental.pallas import tpu as pltpu
from jax.sharding import PartitionSpec as P

HEAD_DIM = 64
TILE_SIDE = 8
WINDOW = 13
GRID_C = 8
PIX = TILE_SIDE * TILE_SIDE
HALF = (WINDOW - 1) // 2
REACH = HALF * TILE_SIDE
SKIP = PIX - REACH
WIDTH = 256
SUB = WIDTH // HEAD_DIM
MASKED = -1e30
F32 = jnp.float32
BF16 = jnp.bfloat16
MESH = pl.DeviceIdType.MESH


def dot(a, b, ca, cb):
    return lax.dot_general(a, b, (((ca,), (cb,)), ((), ())), preferred_element_type=F32)


def fold_rows(x):
    total = x[:PIX]
    for i in range(1, SUB):
        total = total + x[i * PIX : (i + 1) * PIX]
    return total


def kernel(
    count, nv, cols, groups,
    tissue, q_ref, k_ref, v_ref, g_ref, att_ref, dq_ref, dk_ref, dv_ref,
    q_s, g_s, rowx, vertx, bias, drow, dvert, hrow_s, hvert_s, hrow_r, hvert_r, vert_s, vert_r, outs,
    load_sem, store_sem, side_ss, side_rs, up_ss, up_rs, edge_ss, edge_rs,
    hrow_ss, hrow_rs, hvert_ss, hvert_rs, vert_ss, vert_rs,
):
    slide, me = lax.axis_index("slide"), lax.axis_index("row")
    block = lax.rem(me + GRID_C // 2, count)
    grid_row, grid_col = lax.div(block, GRID_C), lax.rem(block, GRID_C)
    block_rows = count // GRID_C

    def at(distance):
        return (slide, lax.rem(me + distance + count, count))

    left, right = at(-1), at(1)
    if nv == 1:
        above = grid_row == 1
        distance = [GRID_C]
        start = [jnp.where(above, 0, SKIP)]
        places = [(jnp.where(above, -1, 1), jnp.where(above, -HALF, TILE_SIDE))]
        seam_left = grid_col == GRID_C // 2
        seam_right = grid_col == GRID_C // 2 - 1
        seam = jnp.logical_or(seam_left, seam_right)
        across = at(jnp.where(seam_left, GRID_C - 1, GRID_C + 1))
    else:
        distance = [GRID_C, -GRID_C]
        start = [jnp.int32(SKIP), jnp.int32(0)]
        places = [(-1, -HALF), (1, TILE_SIDE)]
        seam_left = seam_right = seam = None
    start = [pl.multiple_of(x, 16) for x in start]
    seams = (seam_left, seam_right)

    def lanes(i):
        return pl.ds(pl.multiple_of(i * WIDTH, WIDTH), WIDTH)

    kv = (k_ref, v_ref)
    loads = [pltpu.make_async_copy(x, y, load_sem.at[j]) for j, (x, y) in enumerate((
        (k_ref, rowx.at[0, pl.ds(1, cols)]), (v_ref, rowx.at[1, pl.ds(1, cols)]), (q_ref, q_s), (g_ref, g_s),
    ))]

    def remote(src, dst, ss, rs, device):
        return pltpu.make_async_remote_copy(
            src_ref=src, dst_ref=dst, send_sem=ss, recv_sem=rs, device_id=device, device_id_type=MESH
        )

    def up(i, z, v):
        return remote(
            kv[z].at[:, pl.ds(start[v], REACH), lanes(i)],
            vertx.at[z, v, pl.ds(1, cols), :, lanes(i)],
            up_ss.at[i, z, v], up_rs.at[i, z, v], at(distance[v]),
        )

    def sideways(z, d):
        return remote(
            kv[z].at[0 if d == 0 else cols - 1], rowx.at[z, cols + 1 if d == 0 else 0],
            side_ss.at[z, d], side_rs.at[z, d], left if d == 0 else right,
        )

    def edge(i, z, d):
        return remote(
            vertx.at[z, :, 1 if d == 0 else cols, :, lanes(i)], vertx.at[z, :, cols + 1 if d == 0 else 0, :, lanes(i)],
            edge_ss.at[i, z, d], edge_rs.at[i, z, d], left if d == 0 else right,
        )

    def diagonal(i, z, d):
        return remote(
            kv[z].at[0 if d == 0 else cols - 1, pl.ds(start[0], REACH), lanes(i)],
            vertx.at[z, 0, cols + 1 if d == 0 else 0, :, lanes(i)],
            edge_ss.at[i, z, d], edge_rs.at[i, z, d], across,
        )

    def row_back(i, d):
        return remote(
            hrow_s.at[d, :, :, lanes(i)], hrow_r.at[1 - d, :, :, lanes(i)],
            hrow_ss.at[i, d], hrow_rs.at[i, d], left if d == 0 else right,
        )

    def vert_back(i, d):
        device = left if d == 0 else right
        if seam is not None:
            device = (slide, jnp.where(seams[d], across[1], device[1]))
        return remote(
            hvert_s.at[d, :, :, :, lanes(i)], hvert_r.at[1 - d, :, :, :, lanes(i)],
            hvert_ss.at[i, d], hvert_rs.at[i, d], device,
        )

    def down(i, v):
        return remote(
            vert_s.at[:, v, :, :, lanes(i)], vert_r.at[:, v, :, :, lanes(i)],
            vert_ss.at[i, v], vert_rs.at[i, v], at(-distance[v]),
        )

    def store(i, j):
        return pltpu.make_async_copy(
            outs.at[j, :, :, lanes(i)], (att_ref, dq_ref, dk_ref, dv_ref)[j].at[:, :, lanes(i)], store_sem.at[i, j]
        )

    barrier = pltpu.get_barrier_semaphore()
    for device in [left, right] + [at(x) for x in distance]:
        pl.semaphore_signal(barrier, inc=1, device_id=device, device_id_type=MESH)
    if seam is not None:
        @pl.when(seam)
        def _():
            pl.semaphore_signal(barrier, inc=1, device_id=across, device_id_type=MESH)
    for copy in loads:
        copy.start()
    pl.semaphore_wait(barrier, 2 + nv + (0 if seam is None else seam.astype(jnp.int32)))

    for z in range(2):
        for v in range(nv):
            up(0, z, v).start()
    for z in range(2):
        for d in range(2):
            sideways(z, d).start()
    for i in range(1, groups):
        for z in range(2):
            for v in range(nv):
                up(i, z, v).start()
    if seam is not None:
        for d in range(2):
            @pl.when(seams[d])
            def _():
                for i in range(groups):
                    for z in range(2):
                        diagonal(i, z, d).start()

    query = lax.broadcasted_iota(jnp.int32, (PIX, WIDTH), 1) % PIX
    line = lax.broadcasted_iota(jnp.int32, (PIX, WIDTH), 0)
    top = 0
    for step_row, first, rows in [(0, 0, PIX)] + [(r, f, REACH) for r, f in places]:
        row_gap = first + line[:rows] // TILE_SIDE - query[:rows] // TILE_SIDE
        row = grid_row + step_row
        for step in (-1, 0, 1):
            col_gap = TILE_SIDE * step + line[:rows] % TILE_SIDE - query[:rows] % TILE_SIDE
            near = (jnp.abs(row_gap) <= HALF) & (jnp.abs(col_gap) <= HALF)
            near = jnp.where(near, 0.0, MASKED)
            for c in range(cols):
                col = grid_col * cols + c + step
                inside = (row >= 0) & (row < block_rows) & (col >= 0) & (col < GRID_C * cols)
                flag = tissue[jnp.clip(row, 0, block_rows - 1), jnp.clip(col, 0, GRID_C * cols - 1)]
                shut = jnp.where(inside & (flag > 0), 0.0, MASKED)
                bias[c, top : top + rows] = jnp.minimum(near, shut)
            top += rows
    drow[...] = jnp.zeros_like(drow)
    dvert[...] = jnp.zeros_like(dvert)

    same = (
        lax.broadcasted_iota(jnp.int32, (WIDTH, WIDTH), 0) // PIX
        == lax.broadcasted_iota(jnp.int32, (WIDTH, WIDTH), 1) // HEAD_DIM
    )
    same_low = jnp.where(same, 1.0, 0.0).astype(BF16)

    def keys_of(z, c, i):
        parts = [rowx[z, c : c + 3, :, lanes(i)].reshape(3 * PIX, WIDTH)]
        for v in range(nv):
            parts.append(vertx[z, v, c : c + 3, :, lanes(i)].reshape(3 * REACH, WIDTH))
        return jnp.concatenate(parts, axis=0)

    def attend(i):
        for c in range(cols):
            flag = tissue[grid_row, grid_col * cols + c].astype(F32)
            live = jnp.where(same, flag, 0.0)
            q = q_s[c, :, lanes(i)] * 0.125
            qbd = jnp.concatenate([q] * SUB, axis=0) * same_low
            g = g_s[c, :, lanes(i)]
            gbd = jnp.concatenate([g] * SUB, axis=0) * live.astype(BF16)
            kc, vc = keys_of(0, c, i), keys_of(1, c, i)
            s = dot(kc, qbd, 1, 1) + bias[c]
            peak = jnp.max(s, axis=0, keepdims=True)
            p = jnp.exp(s - peak)
            w = p * (1.0 / jnp.sum(p, axis=0, keepdims=True))
            w_low = w.astype(BF16)
            att_t = (dot(vc, w_low, 0, 0) * live).astype(BF16)
            outs[0, c, :, lanes(i)] = fold_rows(att_t.T)
            out_dot = jnp.sum(att_t.astype(F32) * gbd.T.astype(F32), axis=0, keepdims=True)
            probe = dot(vc, gbd, 1, 1)
            ds = (w * (probe - out_dot)).astype(BF16)
            dq = jnp.where(same, dot(ds, kc, 0, 0), 0.0)
            outs[1, c, :, lanes(i)] = (fold_rows(dq) * 0.125).astype(BF16)
            for z, term in enumerate((dot(ds, qbd, 1, 0), dot(w_low, gbd, 1, 0))):
                drow[z, c : c + 3, :, lanes(i)] += term[: 3 * PIX].reshape(3, PIX, WIDTH)
                for v in range(nv):
                    first = 3 * (PIX + v * REACH)
                    dvert[z, v, c : c + 3, :, lanes(i)] += term[first : first + 3 * REACH].reshape(3, REACH, WIDTH)

    def merge(i):
        for d in range(2):
            row_back(i, d).wait_recv()
            vert_back(i, d).wait_recv()
        for z in range(2):
            for v in range(nv):
                for c in range(cols):
                    vert_s[z, v, c, :, lanes(i)] = dvert[z, v, c + 1, :, lanes(i)].astype(BF16)
        for d, c in ((0, 0), (1, cols - 1)):
            def add(d=d, c=c):
                for z in range(2):
                    for v in range(nv):
                        vert_s[z, v, c, :, lanes(i)] = (
                            dvert[z, v, c + 1, :, lanes(i)] + hvert_r[d, z, v, :, lanes(i)].astype(F32)
                        ).astype(BF16)
            if seam is None:
                add()
            else:
                pl.when(jnp.logical_not(seams[d]))(add)
        for v in range(nv):
            down(i, v).start()

    def step(i, _):
        for z in range(2):
            for v in range(nv):
                up(i, z, v).wait_recv()
        for d in range(2):
            def forward(d=d):
                for z in range(2):
                    edge(i, z, d).start()
            if seam is None:
                forward()
            else:
                pl.when(jnp.logical_not(seams[d]))(forward)

        @pl.when(i > 0)
        def _():
            merge(i - 1)

        @pl.when(i == 0)
        def _():
            for copy in loads:
                copy.wait()
            for z in range(2):
                for d in range(2):
                    sideways(z, d).wait_recv()

        for z in range(2):
            for d in range(2):
                edge(i, z, d).wait_recv()
        attend(i)
        for d, tile in ((0, 0), (1, cols + 1)):
            for z in range(2):
                hrow_s[d, z, :, lanes(i)] = drow[z, tile, :, lanes(i)].astype(BF16)
                for v in range(nv):
                    hvert_s[d, z, v, :, lanes(i)] = dvert[z, v, tile, :, lanes(i)].astype(BF16)
            row_back(i, d).start()
            vert_back(i, d).start()
        for j in range(2):
            store(i, j).start()
        return 0

    lax.fori_loop(0, groups, step, 0)
    merge(groups - 1)

    def finish(i, _):
        for v in range(nv):
            down(i, v).wait_recv()
        for z in range(2):
            drow[z, 1, :, lanes(i)] += hrow_r[0, z, :, lanes(i)].astype(F32)
            drow[z, cols, :, lanes(i)] += hrow_r[1, z, :, lanes(i)].astype(F32)
            for v in range(nv):
                for c in range(cols):
                    drow[z, c + 1, pl.ds(start[v], REACH), lanes(i)] += vert_r[z, v, c, :, lanes(i)].astype(F32)
            if seam is not None:
                for d, c in ((0, 0), (1, cols - 1)):
                    @pl.when(seams[d])
                    def _():
                        drow[z, c + 1, pl.ds(start[0], REACH), lanes(i)] += hvert_r[d, z, 0, :, lanes(i)].astype(F32)
            outs[2 + z, :, :, lanes(i)] = drow[z, 1 : cols + 1, :, lanes(i)].astype(BF16)
            store(i, 2 + z).start()
        return 0

    lax.fori_loop(0, groups, finish, 0)

    def drain(i, _):
        for z in range(2):
            for v in range(nv):
                up(i, z, v).wait_send()
            for d in range(2):
                edge(i, z, d).wait_send()
        for d in range(2):
            row_back(i, d).wait_send()
            vert_back(i, d).wait_send()
        for v in range(nv):
            down(i, v).wait_send()
        for j in range(4):
            store(i, j).wait()
        return 0

    for z in range(2):
        for d in range(2):
            sideways(z, d).wait_send()
    lax.fori_loop(0, groups, drain, 0)


def copy_kernel(*refs):
    sem = refs[-1]
    copies = [pltpu.make_async_copy(refs[j], refs[4 + j], sem.at[j]) for j in range(4)]
    for copy in copies:
        copy.start()
    for copy in copies:
        copy.wait()


def local(query_states, key_states, value_states, grad_output, tissue_map):
    shape = query_states.shape
    cols, inner = shape[2], shape[4]
    q, k, v, g = (x.reshape(cols, PIX, inner) for x in (query_states, key_states, value_states, grad_output))
    count = lax.axis_size("row")
    nv = 1 if count // GRID_C == 2 else 2
    groups = inner // WIDTH
    seen = 3 * (PIX + nv * REACH)
    dma = pltpu.SemaphoreType.DMA
    anywhere = pl.BlockSpec(memory_space=pl.ANY)
    out = pl.pallas_call(
        functools.partial(kernel, count, nv, cols, groups),
        in_specs=[pl.BlockSpec(memory_space=pltpu.SMEM)] + [anywhere] * 4,
        out_specs=[anywhere] * 4,
        out_shape=[jax.ShapeDtypeStruct((cols, PIX, inner), BF16)] * 4,
        scratch_shapes=[
            pltpu.VMEM((cols, PIX, inner), BF16),
            pltpu.VMEM((cols, PIX, inner), BF16),
            pltpu.VMEM((2, cols + 2, PIX, inner), BF16),
            pltpu.VMEM((2, nv, cols + 2, REACH, inner), BF16),
            pltpu.VMEM((cols, seen, WIDTH), F32),
            pltpu.VMEM((2, cols + 2, PIX, inner), F32),
            pltpu.VMEM((2, nv, cols + 2, REACH, inner), F32),
            pltpu.VMEM((2, 2, PIX, inner), BF16),
            pltpu.VMEM((2, 2, nv, REACH, inner), BF16),
            pltpu.VMEM((2, 2, PIX, inner), BF16),
            pltpu.VMEM((2, 2, nv, REACH, inner), BF16),
            pltpu.VMEM((2, nv, cols, REACH, inner), BF16),
            pltpu.VMEM((2, nv, cols, REACH, inner), BF16),
            pltpu.VMEM((4, cols, PIX, inner), BF16),
            dma((4,)), dma((groups, 4)),
            dma((2, 2)), dma((2, 2)),
            dma((groups, 2, nv)), dma((groups, 2, nv)),
            dma((groups, 2, 2)), dma((groups, 2, 2)),
            dma((groups, 2)), dma((groups, 2)),
            dma((groups, 2)), dma((groups, 2)),
            dma((groups, nv)), dma((groups, nv)),
        ],
        compiler_params=pltpu.CompilerParams(
            collective_id=0, has_side_effects=True, vmem_limit_bytes=63 << 20
        ),
        cost_estimate=pl.CostEstimate(
            flops=groups * cols * seen * WIDTH * WIDTH * 2 * 6,
            bytes_accessed=8 << 20,
            transcendentals=groups * cols * seen * WIDTH,
        ),
    )(tissue_map, q, k, v, g)
    out = pl.pallas_call(
        copy_kernel,
        in_specs=[anywhere] * 4,
        out_specs=[anywhere] * 4,
        out_shape=[jax.ShapeDtypeStruct((cols, PIX, inner), BF16)] * 4,
        scratch_shapes=[dma((4,))],
        compiler_params=pltpu.CompilerParams(vmem_limit_bytes=63 << 20),
    )(*out)
    return tuple(x.reshape(shape) for x in out)


def solution(mesh):
    blocks = P(("slide", "row"), None, None, None, None)
    return jax.shard_map(
        local,
        mesh=mesh,
        in_specs=(blocks, blocks, blocks, blocks, P("slide", None)),
        out_specs=(blocks, blocks, blocks, blocks),
        check_vma=False,
    )
```

```python
import functools

import jax
import jax.numpy as jnp
from jax import lax
from jax.experimental import pallas as pl
from jax.experimental.pallas import tpu as pltpu
from jax.sharding import PartitionSpec as P

HEAD_DIM = 64
TILE_SIDE = 8
WINDOW = 13
GRID_C = 8
PIX = TILE_SIDE * TILE_SIDE
HALF = (WINDOW - 1) // 2
REACH = HALF * TILE_SIDE
SKIP = PIX - REACH
WIDTH = 256
SUB = WIDTH // HEAD_DIM
MASKED = -1e30
F32 = jnp.float32
BF16 = jnp.bfloat16
MESH = pl.DeviceIdType.MESH


def dot(a, b, ca, cb):
    return lax.dot_general(a, b, (((ca,), (cb,)), ((), ())), preferred_element_type=F32)


def fold_rows(x):
    total = x[:PIX]
    for i in range(1, SUB):
        total = total + x[i * PIX : (i + 1) * PIX]
    return total


def kernel(
    count, nv, cols, groups,
    tissue, q_ref, k_ref, v_ref, g_ref, att_ref, dq_ref, dk_ref, dv_ref,
    q_s, g_s, rowx, vertx, bias, drow, dvert, hrow_s, hvert_s, hrow_r, hvert_r, vert_s, vert_r, outs,
    load_sem, store_sem, side_ss, side_rs, up_ss, up_rs, edge_ss, edge_rs,
    hrow_ss, hrow_rs, hvert_ss, hvert_rs, vert_ss, vert_rs,
):
    slide, me = lax.axis_index("slide"), lax.axis_index("row")
    block = lax.rem(me + GRID_C // 2, count)
    grid_row, grid_col = lax.div(block, GRID_C), lax.rem(block, GRID_C)
    block_rows = count // GRID_C

    def at(distance):
        return (slide, lax.rem(me + distance + count, count))

    left, right = at(-1), at(1)
    if nv == 1:
        above = grid_row == 1
        distance = [GRID_C]
        start = [jnp.where(above, 0, SKIP)]
        places = [(jnp.where(above, -1, 1), jnp.where(above, -HALF, TILE_SIDE))]
        seam_left = grid_col == GRID_C // 2
        seam_right = grid_col == GRID_C // 2 - 1
        seam = jnp.logical_or(seam_left, seam_right)
        across = at(jnp.where(seam_left, GRID_C - 1, GRID_C + 1))
    else:
        distance = [GRID_C, -GRID_C]
        start = [jnp.int32(SKIP), jnp.int32(0)]
        places = [(-1, -HALF), (1, TILE_SIDE)]
        seam_left = seam_right = seam = None
    start = [pl.multiple_of(x, 16) for x in start]
    seams = (seam_left, seam_right)

    def lanes(i):
        return pl.ds(pl.multiple_of(i * WIDTH, WIDTH), WIDTH)

    kv = (k_ref, v_ref)
    loads = [pltpu.make_async_copy(x, y, load_sem.at[j]) for j, (x, y) in enumerate((
        (k_ref, rowx.at[0, pl.ds(1, cols)]), (v_ref, rowx.at[1, pl.ds(1, cols)]), (q_ref, q_s), (g_ref, g_s),
    ))]

    def remote(src, dst, ss, rs, device):
        return pltpu.make_async_remote_copy(
            src_ref=src, dst_ref=dst, send_sem=ss, recv_sem=rs, device_id=device, device_id_type=MESH
        )

    def up(i, z, v):
        return remote(
            kv[z].at[:, pl.ds(start[v], REACH), lanes(i)],
            vertx.at[z, v, pl.ds(1, cols), :, lanes(i)],
            up_ss.at[i, z, v], up_rs.at[i, z, v], at(distance[v]),
        )

    def sideways(z, d):
        return remote(
            kv[z].at[0 if d == 0 else cols - 1], rowx.at[z, cols + 1 if d == 0 else 0],
            side_ss.at[z, d], side_rs.at[z, d], left if d == 0 else right,
        )

    def edge(i, z, d):
        return remote(
            vertx.at[z, :, 1 if d == 0 else cols, :, lanes(i)], vertx.at[z, :, cols + 1 if d == 0 else 0, :, lanes(i)],
            edge_ss.at[i, z, d], edge_rs.at[i, z, d], left if d == 0 else right,
        )

    def diagonal(i, z, d):
        return remote(
            kv[z].at[0 if d == 0 else cols - 1, pl.ds(start[0], REACH), lanes(i)],
            vertx.at[z, 0, cols + 1 if d == 0 else 0, :, lanes(i)],
            edge_ss.at[i, z, d], edge_rs.at[i, z, d], across,
        )

    def row_back(i, d):
        return remote(
            hrow_s.at[d, :, :, lanes(i)], hrow_r.at[1 - d, :, :, lanes(i)],
            hrow_ss.at[i, d], hrow_rs.at[i, d], left if d == 0 else right,
        )

    def vert_back(i, d):
        device = left if d == 0 else right
        if seam is not None:
            device = (slide, jnp.where(seams[d], across[1], device[1]))
        return remote(
            hvert_s.at[d, :, :, :, lanes(i)], hvert_r.at[1 - d, :, :, :, lanes(i)],
            hvert_ss.at[i, d], hvert_rs.at[i, d], device,
        )

    def down(i, v):
        return remote(
            vert_s.at[:, v, :, :, lanes(i)], vert_r.at[:, v, :, :, lanes(i)],
            vert_ss.at[i, v], vert_rs.at[i, v], at(-distance[v]),
        )

    def store(i, j):
        return pltpu.make_async_copy(
            outs.at[j, :, :, lanes(i)], (att_ref, dq_ref, dk_ref, dv_ref)[j].at[:, :, lanes(i)], store_sem.at[i, j]
        )

    barrier = pltpu.get_barrier_semaphore()
    for device in [left, right] + [at(x) for x in distance]:
        pl.semaphore_signal(barrier, inc=1, device_id=device, device_id_type=MESH)
    if seam is not None:
        @pl.when(seam)
        def _():
            pl.semaphore_signal(barrier, inc=1, device_id=across, device_id_type=MESH)
    for copy in loads:
        copy.start()
    pl.semaphore_wait(barrier, 2 + nv + (0 if seam is None else seam.astype(jnp.int32)))

    for z in range(2):
        for v in range(nv):
            up(0, z, v).start()
    for z in range(2):
        for d in range(2):
            sideways(z, d).start()
    for i in range(1, groups):
        for z in range(2):
            for v in range(nv):
                up(i, z, v).start()
    if seam is not None:
        for d in range(2):
            @pl.when(seams[d])
            def _():
                for i in range(groups):
                    for z in range(2):
                        diagonal(i, z, d).start()

    query = lax.broadcasted_iota(jnp.int32, (PIX, WIDTH), 1) % PIX
    line = lax.broadcasted_iota(jnp.int32, (PIX, WIDTH), 0)
    top = 0
    for step_row, first, rows in [(0, 0, PIX)] + [(r, f, REACH) for r, f in places]:
        row_gap = first + line[:rows] // TILE_SIDE - query[:rows] // TILE_SIDE
        row = grid_row + step_row
        for step in (-1, 0, 1):
            col_gap = TILE_SIDE * step + line[:rows] % TILE_SIDE - query[:rows] % TILE_SIDE
            near = (jnp.abs(row_gap) <= HALF) & (jnp.abs(col_gap) <= HALF)
            near = jnp.where(near, 0.0, MASKED)
            for c in range(cols):
                col = grid_col * cols + c + step
                inside = (row >= 0) & (row < block_rows) & (col >= 0) & (col < GRID_C * cols)
                flag = tissue[jnp.clip(row, 0, block_rows - 1), jnp.clip(col, 0, GRID_C * cols - 1)]
                shut = jnp.where(inside & (flag > 0), 0.0, MASKED)
                bias[c, top : top + rows] = jnp.minimum(near, shut)
            top += rows
    drow[...] = jnp.zeros_like(drow)
    dvert[...] = jnp.zeros_like(dvert)

    same = (
        lax.broadcasted_iota(jnp.int32, (WIDTH, WIDTH), 0) // PIX
        == lax.broadcasted_iota(jnp.int32, (WIDTH, WIDTH), 1) // HEAD_DIM
    )
    same_low = jnp.where(same, 1.0, 0.0).astype(BF16)

    def keys_of(z, c, i):
        parts = [rowx[z, c : c + 3, :, lanes(i)].reshape(3 * PIX, WIDTH)]
        for v in range(nv):
            parts.append(vertx[z, v, c : c + 3, :, lanes(i)].reshape(3 * REACH, WIDTH))
        return jnp.concatenate(parts, axis=0)

    def attend(i):
        for c in range(cols):
            flag = tissue[grid_row, grid_col * cols + c].astype(F32)
            live = jnp.where(same, flag, 0.0)
            q = q_s[c, :, lanes(i)] * 0.125
            qbd = jnp.concatenate([q] * SUB, axis=0) * same_low
            g = g_s[c, :, lanes(i)]
            gbd = jnp.concatenate([g] * SUB, axis=0) * live.astype(BF16)
            kc, vc = keys_of(0, c, i), keys_of(1, c, i)
            s = dot(kc, qbd, 1, 1) + bias[c]
            peak = jnp.max(s, axis=0, keepdims=True)
            p = jnp.exp(s - peak)
            w = p * (1.0 / jnp.sum(p, axis=0, keepdims=True))
            w_low = w.astype(BF16)
            att_t = (dot(vc, w_low, 0, 0) * live).astype(BF16)
            outs[0, c, :, lanes(i)] = fold_rows(att_t.T)
            out_dot = jnp.sum(att_t.astype(F32) * gbd.T.astype(F32), axis=0, keepdims=True)
            probe = dot(vc, gbd, 1, 1)
            ds = (w * (probe - out_dot)).astype(BF16)
            dq = jnp.where(same, dot(ds, kc, 0, 0), 0.0)
            outs[1, c, :, lanes(i)] = (fold_rows(dq) * 0.125).astype(BF16)
            for z, term in enumerate((dot(ds, qbd, 1, 0), dot(w_low, gbd, 1, 0))):
                drow[z, c : c + 3, :, lanes(i)] += term[: 3 * PIX].reshape(3, PIX, WIDTH)
                for v in range(nv):
                    first = 3 * (PIX + v * REACH)
                    dvert[z, v, c : c + 3, :, lanes(i)] += term[first : first + 3 * REACH].reshape(3, REACH, WIDTH)

    def merge(i):
        for d in range(2):
            row_back(i, d).wait_recv()
            vert_back(i, d).wait_recv()
        for z in range(2):
            for v in range(nv):
                for c in range(cols):
                    vert_s[z, v, c, :, lanes(i)] = dvert[z, v, c + 1, :, lanes(i)].astype(BF16)
        for d, c in ((0, 0), (1, cols - 1)):
            def add(d=d, c=c):
                for z in range(2):
                    for v in range(nv):
                        vert_s[z, v, c, :, lanes(i)] = (
                            dvert[z, v, c + 1, :, lanes(i)] + hvert_r[d, z, v, :, lanes(i)].astype(F32)
                        ).astype(BF16)
            if seam is None:
                add()
            else:
                pl.when(jnp.logical_not(seams[d]))(add)
        for v in range(nv):
            down(i, v).start()

    def step(i, _):
        for z in range(2):
            for v in range(nv):
                up(i, z, v).wait_recv()
        for d in range(2):
            def forward(d=d):
                for z in range(2):
                    edge(i, z, d).start()
            if seam is None:
                forward()
            else:
                pl.when(jnp.logical_not(seams[d]))(forward)

        @pl.when(i > 0)
        def _():
            merge(i - 1)

        @pl.when(i == 0)
        def _():
            for copy in loads:
                copy.wait()
            for z in range(2):
                for d in range(2):
                    sideways(z, d).wait_recv()

        for z in range(2):
            for d in range(2):
                edge(i, z, d).wait_recv()
        attend(i)
        for d, tile in ((0, 0), (1, cols + 1)):
            for z in range(2):
                hrow_s[d, z, :, lanes(i)] = drow[z, tile, :, lanes(i)].astype(BF16)
                for v in range(nv):
                    hvert_s[d, z, v, :, lanes(i)] = dvert[z, v, tile, :, lanes(i)].astype(BF16)
            row_back(i, d).start()
            vert_back(i, d).start()
        for j in range(2):
            store(i, j).start()
        return 0

    lax.fori_loop(0, groups, step, 0)
    merge(groups - 1)

    def finish(i, _):
        for v in range(nv):
            down(i, v).wait_recv()
        for z in range(2):
            drow[z, 1, :, lanes(i)] += hrow_r[0, z, :, lanes(i)].astype(F32)
            drow[z, cols, :, lanes(i)] += hrow_r[1, z, :, lanes(i)].astype(F32)
            for v in range(nv):
                for c in range(cols):
                    drow[z, c + 1, pl.ds(start[v], REACH), lanes(i)] += vert_r[z, v, c, :, lanes(i)].astype(F32)
            if seam is not None:
                for d, c in ((0, 0), (1, cols - 1)):
                    @pl.when(seams[d])
                    def _():
                        drow[z, c + 1, pl.ds(start[0], REACH), lanes(i)] += hvert_r[d, z, 0, :, lanes(i)].astype(F32)
            outs[2 + z, :, :, lanes(i)] = drow[z, 1 : cols + 1, :, lanes(i)].astype(BF16)
            store(i, 2 + z).start()
        return 0

    lax.fori_loop(0, groups, finish, 0)

    def drain(i, _):
        for z in range(2):
            for v in range(nv):
                up(i, z, v).wait_send()
            for d in range(2):
                edge(i, z, d).wait_send()
        for d in range(2):
            row_back(i, d).wait_send()
            vert_back(i, d).wait_send()
        for v in range(nv):
            down(i, v).wait_send()
        for j in range(4):
            store(i, j).wait()
        return 0

    for z in range(2):
        for d in range(2):
            sideways(z, d).wait_send()
    lax.fori_loop(0, groups, drain, 0)


def copy_kernel(*refs):
    sem = refs[-1]
    copies = [pltpu.make_async_copy(refs[j], refs[4 + j], sem.at[j]) for j in range(4)]
    for copy in copies:
        copy.start()
    for copy in copies:
        copy.wait()


def local(query_states, key_states, value_states, grad_output, tissue_map):
    shape = query_states.shape
    cols, inner = shape[2], shape[4]
    q, k, v, g = (x.reshape(cols, PIX, inner) for x in (query_states, key_states, value_states, grad_output))
    count = lax.axis_size("row")
    nv = 1 if count // GRID_C == 2 else 2
    groups = inner // WIDTH
    seen = 3 * (PIX + nv * REACH)
    dma = pltpu.SemaphoreType.DMA
    anywhere = pl.BlockSpec(memory_space=pl.ANY)
    out = pl.pallas_call(
        functools.partial(kernel, count, nv, cols, groups),
        in_specs=[pl.BlockSpec(memory_space=pltpu.SMEM)] + [anywhere] * 4,
        out_specs=[anywhere] * 4,
        out_shape=[jax.ShapeDtypeStruct((cols, PIX, inner), BF16)] * 4,
        scratch_shapes=[
            pltpu.VMEM((cols, PIX, inner), BF16),
            pltpu.VMEM((cols, PIX, inner), BF16),
            pltpu.VMEM((2, cols + 2, PIX, inner), BF16),
            pltpu.VMEM((2, nv, cols + 2, REACH, inner), BF16),
            pltpu.VMEM((cols, seen, WIDTH), F32),
            pltpu.VMEM((2, cols + 2, PIX, inner), F32),
            pltpu.VMEM((2, nv, cols + 2, REACH, inner), F32),
            pltpu.VMEM((2, 2, PIX, inner), BF16),
            pltpu.VMEM((2, 2, nv, REACH, inner), BF16),
            pltpu.VMEM((2, 2, PIX, inner), BF16),
            pltpu.VMEM((2, 2, nv, REACH, inner), BF16),
            pltpu.VMEM((2, nv, cols, REACH, inner), BF16),
            pltpu.VMEM((2, nv, cols, REACH, inner), BF16),
            pltpu.VMEM((4, cols, PIX, inner), BF16),
            dma((4,)), dma((groups, 4)),
            dma((2, 2)), dma((2, 2)),
            dma((groups, 2, nv)), dma((groups, 2, nv)),
            dma((groups, 2, 2)), dma((groups, 2, 2)),
            dma((groups, 2)), dma((groups, 2)),
            dma((groups, 2)), dma((groups, 2)),
            dma((groups, nv)), dma((groups, nv)),
        ],
        compiler_params=pltpu.CompilerParams(
            collective_id=0, has_side_effects=True, vmem_limit_bytes=54787072
        ),
        cost_estimate=pl.CostEstimate(
            flops=groups * cols * seen * WIDTH * WIDTH * 2 * 6,
            bytes_accessed=8 << 20,
            transcendentals=groups * cols * seen * WIDTH,
        ),
    )(tissue_map, q, k, v, g)
    out = pl.pallas_call(
        copy_kernel,
        in_specs=[anywhere] * 4,
        out_specs=[anywhere] * 4,
        out_shape=[jax.ShapeDtypeStruct((cols, PIX, inner), BF16)] * 4,
        scratch_shapes=[dma((4,))],
        compiler_params=pltpu.CompilerParams(vmem_limit_bytes=54787072),
    )(*out)
    return tuple(x.reshape(shape) for x in out)


def solution(mesh):
    blocks = P(("slide", "row"), None, None, None, None)
    return jax.shard_map(
        local,
        mesh=mesh,
        in_specs=(blocks, blocks, blocks, blocks, P("slide", None)),
        out_specs=(blocks, blocks, blocks, blocks),
        check_vma=False,
    )
```

```python
import functools

import jax
import jax.numpy as jnp
from jax import lax
from jax.experimental import pallas as pl
from jax.experimental.pallas import tpu as pltpu
from jax.sharding import PartitionSpec as P

HEAD_DIM = 64
TILE_SIDE = 8
WINDOW = 13
GRID_C = 8
PIX = TILE_SIDE * TILE_SIDE
HALF = (WINDOW - 1) // 2
REACH = HALF * TILE_SIDE
SKIP = PIX - REACH
WIDTH = 256
SUB = WIDTH // HEAD_DIM
MASKED = -1e30
F32 = jnp.float32
BF16 = jnp.bfloat16
MESH = pl.DeviceIdType.MESH


def dot(a, b, ca, cb):
    return lax.dot_general(a, b, (((ca,), (cb,)), ((), ())), preferred_element_type=F32)


def fold_rows(x):
    total = x[:PIX]
    for i in range(1, SUB):
        total = total + x[i * PIX : (i + 1) * PIX]
    return total


def kernel(
    count, nv, cols, groups,
    tissue, q_ref, k_ref, v_ref, g_ref, att_ref, dq_ref, dk_ref, dv_ref,
    q_s, g_s, rowx, vertx, bias, drow, dvert, hrow_s, hvert_s, hrow_r, hvert_r, relay_r, vert_s, vert_r, outs,
    load_sem, store_sem, side_ss, side_rs, up_ss, up_rs, edge_ss, edge_rs,
    hrow_ss, hrow_rs, hvert_ss, hvert_rs, vert_ss, vert_rs, relay_ss, relay_rs, relay_back_ss, relay_back_rs,
):
    slide, me = lax.axis_index("slide"), lax.axis_index("row")
    block = lax.rem(me + GRID_C // 2, count)
    grid_row, grid_col = lax.div(block, GRID_C), lax.rem(block, GRID_C)
    block_rows = count // GRID_C

    def at(distance):
        return (slide, lax.rem(me + distance + count, count))

    left, right = at(-1), at(1)
    if nv == 1:
        above = grid_row == 1
        distance = [GRID_C]
        start = [jnp.where(above, 0, SKIP)]
        places = [(jnp.where(above, -1, 1), jnp.where(above, -HALF, TILE_SIDE))]
        seam_left = grid_col == GRID_C // 2
        seam_right = grid_col == GRID_C // 2 - 1
        seam = jnp.logical_or(seam_left, seam_right)
        across = at(jnp.where(seam_left, GRID_C - 1, GRID_C + 1))
    else:
        distance = [GRID_C, -GRID_C]
        start = [jnp.int32(SKIP), jnp.int32(0)]
        places = [(-1, -HALF), (1, TILE_SIDE)]
        seam_left = seam_right = seam = None
    start = [pl.multiple_of(x, 16) for x in start]
    seams = (seam_left, seam_right)
    if seam is not None:
        start_other = pl.multiple_of(SKIP - start[0], 16)
        rest = pl.multiple_of(jnp.where(above, REACH, 0), 16)

    def lanes(i):
        return pl.ds(pl.multiple_of(i * WIDTH, WIDTH), WIDTH)

    kv = (k_ref, v_ref)
    loads = [pltpu.make_async_copy(x, y, load_sem.at[j]) for j, (x, y) in enumerate((
        (k_ref, rowx.at[0, pl.ds(1, cols)]), (v_ref, rowx.at[1, pl.ds(1, cols)]), (q_ref, q_s), (g_ref, g_s),
    ))]

    def remote(src, dst, ss, rs, device):
        return pltpu.make_async_remote_copy(
            src_ref=src, dst_ref=dst, send_sem=ss, recv_sem=rs, device_id=device, device_id_type=MESH
        )

    def up(i, z, v):
        return remote(
            kv[z].at[:, pl.ds(start[v], REACH), lanes(i)],
            vertx.at[z, v, pl.ds(1, cols), :, lanes(i)],
            up_ss.at[i, z, v], up_rs.at[i, z, v], at(distance[v]),
        )

    def sideways(z, d, seamed=False):
        src, dst = kv[z].at[0 if d == 0 else cols - 1], rowx.at[z, cols + 1 if d == 0 else 0]
        if seamed:
            src, dst = src.at[pl.ds(rest, SKIP)], dst.at[pl.ds(rest, SKIP)]
        return remote(src, dst, side_ss.at[z, d], side_rs.at[z, d], left if d == 0 else right)

    def relay(i, z, d):
        return remote(
            vertx.at[z, 0, 1 if d == 0 else cols, :, lanes(i)],
            rowx.at[z, cols + 1 if d == 0 else 0, pl.ds(start_other, REACH), lanes(i)],
            relay_ss.at[i, z], relay_rs.at[i, z], across,
        )

    def by_seam(d, run):
        if seam is None:
            run(False)
        else:
            pl.when(seams[d])(lambda: run(True))
            pl.when(jnp.logical_not(seams[d]))(lambda: run(False))

    def edge(i, z, d):
        return remote(
            vertx.at[z, :, 1 if d == 0 else cols, :, lanes(i)], vertx.at[z, :, cols + 1 if d == 0 else 0, :, lanes(i)],
            edge_ss.at[i, z, d], edge_rs.at[i, z, d], left if d == 0 else right,
        )

    def diagonal(i, z, d):
        return remote(
            kv[z].at[0 if d == 0 else cols - 1, pl.ds(start[0], REACH), lanes(i)],
            vertx.at[z, 0, cols + 1 if d == 0 else 0, :, lanes(i)],
            edge_ss.at[i, z, d], edge_rs.at[i, z, d], across,
        )

    def row_back(i, d, seamed=False):
        rows = pl.ds(rest, SKIP) if seamed else slice(None)
        return remote(
            hrow_s.at[d, :, rows, lanes(i)], hrow_r.at[1 - d, :, rows, lanes(i)],
            hrow_ss.at[i, d], hrow_rs.at[i, d], left if d == 0 else right,
        )

    def relay_back(i, d):
        return remote(
            hrow_s.at[d, :, pl.ds(start[0], REACH), lanes(i)], relay_r.at[:, :, lanes(i)],
            relay_back_ss.at[i], relay_back_rs.at[i], across,
        )

    def vert_back(i, d):
        device = left if d == 0 else right
        if seam is not None:
            device = (slide, jnp.where(seams[d], across[1], device[1]))
        return remote(
            hvert_s.at[d, :, :, :, lanes(i)], hvert_r.at[1 - d, :, :, :, lanes(i)],
            hvert_ss.at[i, d], hvert_rs.at[i, d], device,
        )

    def down(i, v):
        return remote(
            vert_s.at[:, v, :, :, lanes(i)], vert_r.at[:, v, :, :, lanes(i)],
            vert_ss.at[i, v], vert_rs.at[i, v], at(-distance[v]),
        )

    def store(i, j):
        return pltpu.make_async_copy(
            outs.at[j, :, :, lanes(i)], (att_ref, dq_ref, dk_ref, dv_ref)[j].at[:, :, lanes(i)], store_sem.at[i, j]
        )

    barrier = pltpu.get_barrier_semaphore()
    for device in [left, right] + [at(x) for x in distance]:
        pl.semaphore_signal(barrier, inc=1, device_id=device, device_id_type=MESH)
    if seam is not None:
        @pl.when(seam)
        def _():
            pl.semaphore_signal(barrier, inc=1, device_id=across, device_id_type=MESH)
    for copy in loads:
        copy.start()
    pl.semaphore_wait(barrier, 2 + nv + (0 if seam is None else seam.astype(jnp.int32)))

    for z in range(2):
        for v in range(nv):
            up(0, z, v).start()
    for d in range(2):
        def send(seamed, d=d):
            for z in range(2):
                sideways(z, d, seamed).start()
        by_seam(d, send)
    for i in range(1, groups):
        for z in range(2):
            for v in range(nv):
                up(i, z, v).start()
    if seam is not None:
        for d in range(2):
            @pl.when(seams[d])
            def _():
                for i in range(groups):
                    for z in range(2):
                        diagonal(i, z, d).start()

    query = lax.broadcasted_iota(jnp.int32, (PIX, WIDTH), 1) % PIX
    line = lax.broadcasted_iota(jnp.int32, (PIX, WIDTH), 0)
    top = 0
    for step_row, first, rows in [(0, 0, PIX)] + [(r, f, REACH) for r, f in places]:
        row_gap = first + line[:rows] // TILE_SIDE - query[:rows] // TILE_SIDE
        row = grid_row + step_row
        for step in (-1, 0, 1):
            col_gap = TILE_SIDE * step + line[:rows] % TILE_SIDE - query[:rows] % TILE_SIDE
            near = (jnp.abs(row_gap) <= HALF) & (jnp.abs(col_gap) <= HALF)
            near = jnp.where(near, 0.0, MASKED)
            for c in range(cols):
                col = grid_col * cols + c + step
                inside = (row >= 0) & (row < block_rows) & (col >= 0) & (col < GRID_C * cols)
                flag = tissue[jnp.clip(row, 0, block_rows - 1), jnp.clip(col, 0, GRID_C * cols - 1)]
                shut = jnp.where(inside & (flag > 0), 0.0, MASKED)
                bias[c, top : top + rows] = jnp.minimum(near, shut)
            top += rows
    drow[...] = jnp.zeros_like(drow)
    dvert[...] = jnp.zeros_like(dvert)

    same = (
        lax.broadcasted_iota(jnp.int32, (WIDTH, WIDTH), 0) // PIX
        == lax.broadcasted_iota(jnp.int32, (WIDTH, WIDTH), 1) // HEAD_DIM
    )
    same_low = jnp.where(same, 1.0, 0.0).astype(BF16)

    def keys_of(z, c, i):
        parts = [rowx[z, c : c + 3, :, lanes(i)].reshape(3 * PIX, WIDTH)]
        for v in range(nv):
            parts.append(vertx[z, v, c : c + 3, :, lanes(i)].reshape(3 * REACH, WIDTH))
        return jnp.concatenate(parts, axis=0)

    def attend(i):
        for c in range(cols):
            flag = tissue[grid_row, grid_col * cols + c].astype(F32)
            live = jnp.where(same, flag, 0.0)
            q = q_s[c, :, lanes(i)] * 0.125
            qbd = jnp.concatenate([q] * SUB, axis=0) * same_low
            g = g_s[c, :, lanes(i)]
            gbd = jnp.concatenate([g] * SUB, axis=0) * live.astype(BF16)
            kc, vc = keys_of(0, c, i), keys_of(1, c, i)
            s = dot(kc, qbd, 1, 1) + bias[c]
            peak = jnp.max(s, axis=0, keepdims=True)
            p = jnp.exp(s - peak)
            w = p * (1.0 / jnp.sum(p, axis=0, keepdims=True))
            w_low = w.astype(BF16)
            att_t = (dot(vc, w_low, 0, 0) * live).astype(BF16)
            outs[0, c, :, lanes(i)] = fold_rows(att_t.T)
            out_dot = jnp.sum(att_t.astype(F32) * gbd.T.astype(F32), axis=0, keepdims=True)
            probe = dot(vc, gbd, 1, 1)
            ds = (w * (probe - out_dot)).astype(BF16)
            dq = jnp.where(same, dot(ds, kc, 0, 0), 0.0)
            outs[1, c, :, lanes(i)] = (fold_rows(dq) * 0.125).astype(BF16)
            for z, term in enumerate((dot(ds, qbd, 1, 0), dot(w_low, gbd, 1, 0))):
                drow[z, c : c + 3, :, lanes(i)] += term[: 3 * PIX].reshape(3, PIX, WIDTH)
                for v in range(nv):
                    first = 3 * (PIX + v * REACH)
                    dvert[z, v, c : c + 3, :, lanes(i)] += term[first : first + 3 * REACH].reshape(3, REACH, WIDTH)

    def merge(i):
        for d in range(2):
            vert_back(i, d).wait_recv()
        if seam is not None:
            @pl.when(seam)
            def _():
                relay_back(i, 0).wait_recv()
        for z in range(2):
            for v in range(nv):
                for c in range(cols):
                    vert_s[z, v, c, :, lanes(i)] = dvert[z, v, c + 1, :, lanes(i)].astype(BF16)
        for d, c in ((0, 0), (1, cols - 1)):
            def add(seamed, d=d, c=c):
                for z in range(2):
                    for v in range(nv):
                        edge_term = relay_r[z, :, lanes(i)] if seamed else hvert_r[d, z, v, :, lanes(i)]
                        vert_s[z, v, c, :, lanes(i)] = (
                            dvert[z, v, c + 1, :, lanes(i)] + edge_term.astype(F32)
                        ).astype(BF16)
            by_seam(d, add)
        for v in range(nv):
            down(i, v).start()

    def step(i, _):
        for z in range(2):
            for v in range(nv):
                up(i, z, v).wait_recv()
        for d in range(2):
            def forward(seamed, d=d):
                for z in range(2):
                    (relay if seamed else edge)(i, z, d).start()
            by_seam(d, forward)

        @pl.when(i > 0)
        def _():
            merge(i - 1)

        @pl.when(i == 0)
        def _():
            for copy in loads:
                copy.wait()
            for d in range(2):
                def wait(seamed, d=d):
                    for z in range(2):
                        sideways(z, d, seamed).wait_recv()
                by_seam(1 - d, wait)

        for z in range(2):
            for d in range(2):
                edge(i, z, d).wait_recv()
        if seam is not None:
            for d in range(2):
                @pl.when(seams[1 - d])
                def _():
                    for z in range(2):
                        relay(i, z, d).wait_recv()
        attend(i)
        for d, tile in ((0, 0), (1, cols + 1)):
            for z in range(2):
                hrow_s[d, z, :, lanes(i)] = drow[z, tile, :, lanes(i)].astype(BF16)
                for v in range(nv):
                    hvert_s[d, z, v, :, lanes(i)] = dvert[z, v, tile, :, lanes(i)].astype(BF16)
            def give(seamed, d=d):
                if seamed:
                    relay_back(i, d).start()
                row_back(i, d, seamed).start()
            vert_back(i, d).start()
            by_seam(d, give)
        for j in range(2):
            store(i, j).start()
        return 0

    lax.fori_loop(0, groups, step, 0)
    merge(groups - 1)

    def finish(i, _):
        for v in range(nv):
            down(i, v).wait_recv()
        for d, c in ((1, 0), (0, cols - 1)):
            def add(seamed, d=d, c=c):
                row_back(i, d, seamed).wait_recv()
                rows = pl.ds(rest, SKIP) if seamed else slice(None)
                for z in range(2):
                    drow[z, c + 1, rows, lanes(i)] += hrow_r[1 - d, z, rows, lanes(i)].astype(F32)
            by_seam(1 - d, add)
        for z in range(2):
            for v in range(nv):
                for c in range(cols):
                    drow[z, c + 1, pl.ds(start[v], REACH), lanes(i)] += vert_r[z, v, c, :, lanes(i)].astype(F32)
            if seam is not None:
                for d, c in ((0, 0), (1, cols - 1)):
                    @pl.when(seams[d])
                    def _():
                        drow[z, c + 1, pl.ds(start[0], REACH), lanes(i)] += hvert_r[d, z, 0, :, lanes(i)].astype(F32)
            outs[2 + z, :, :, lanes(i)] = drow[z, 1 : cols + 1, :, lanes(i)].astype(BF16)
            store(i, 2 + z).start()
        return 0

    lax.fori_loop(0, groups, finish, 0)

    def drain(i, _):
        for z in range(2):
            for v in range(nv):
                up(i, z, v).wait_send()
            for d in range(2):
                edge(i, z, d).wait_send()
        if seam is not None:
            for d in range(2):
                @pl.when(seams[d])
                def _():
                    for z in range(2):
                        relay(i, z, d).wait_send()
        for d in range(2):
            def sent(seamed, d=d):
                if seamed:
                    relay_back(i, d).wait_send()
                row_back(i, d, seamed).wait_send()
            vert_back(i, d).wait_send()
            by_seam(d, sent)
        for v in range(nv):
            down(i, v).wait_send()
        for j in range(4):
            store(i, j).wait()
        return 0

    for d in range(2):
        def sent(seamed, d=d):
            for z in range(2):
                sideways(z, d, seamed).wait_send()
        by_seam(d, sent)
    lax.fori_loop(0, groups, drain, 0)


def copy_kernel(*refs):
    sem = refs[-1]
    copies = [pltpu.make_async_copy(refs[j], refs[4 + j], sem.at[j]) for j in range(4)]
    for copy in copies:
        copy.start()
    for copy in copies:
        copy.wait()


def local(query_states, key_states, value_states, grad_output, tissue_map):
    shape = query_states.shape
    cols, inner = shape[2], shape[4]
    q, k, v, g = (x.reshape(cols, PIX, inner) for x in (query_states, key_states, value_states, grad_output))
    count = lax.axis_size("row")
    nv = 1 if count // GRID_C == 2 else 2
    groups = inner // WIDTH
    seen = 3 * (PIX + nv * REACH)
    dma = pltpu.SemaphoreType.DMA
    anywhere = pl.BlockSpec(memory_space=pl.ANY)
    out = pl.pallas_call(
        functools.partial(kernel, count, nv, cols, groups),
        in_specs=[pl.BlockSpec(memory_space=pltpu.SMEM)] + [anywhere] * 4,
        out_specs=[anywhere] * 4,
        out_shape=[jax.ShapeDtypeStruct((cols, PIX, inner), BF16)] * 4,
        scratch_shapes=[
            pltpu.VMEM((cols, PIX, inner), BF16),
            pltpu.VMEM((cols, PIX, inner), BF16),
            pltpu.VMEM((2, cols + 2, PIX, inner), BF16),
            pltpu.VMEM((2, nv, cols + 2, REACH, inner), BF16),
            pltpu.VMEM((cols, seen, WIDTH), F32),
            pltpu.VMEM((2, cols + 2, PIX, inner), F32),
            pltpu.VMEM((2, nv, cols + 2, REACH, inner), F32),
            pltpu.VMEM((2, 2, PIX, inner), BF16),
            pltpu.VMEM((2, 2, nv, REACH, inner), BF16),
            pltpu.VMEM((2, 2, PIX, inner), BF16),
            pltpu.VMEM((2, 2, nv, REACH, inner), BF16),
            pltpu.VMEM((2, REACH, inner), BF16),
            pltpu.VMEM((2, nv, cols, REACH, inner), BF16),
            pltpu.VMEM((2, nv, cols, REACH, inner), BF16),
            pltpu.VMEM((4, cols, PIX, inner), BF16),
            dma((4,)), dma((groups, 4)),
            dma((2, 2)), dma((2, 2)),
            dma((groups, 2, nv)), dma((groups, 2, nv)),
            dma((groups, 2, 2)), dma((groups, 2, 2)),
            dma((groups, 2)), dma((groups, 2)),
            dma((groups, 2)), dma((groups, 2)),
            dma((groups, nv)), dma((groups, nv)),
            dma((groups, 2)), dma((groups, 2)), dma((groups,)), dma((groups,)),
        ],
        compiler_params=pltpu.CompilerParams(
            collective_id=0, has_side_effects=True, vmem_limit_bytes=54787072
        ),
        cost_estimate=pl.CostEstimate(
            flops=groups * cols * seen * WIDTH * WIDTH * 2 * 6,
            bytes_accessed=8 << 20,
            transcendentals=groups * cols * seen * WIDTH,
        ),
    )(tissue_map, q, k, v, g)
    out = pl.pallas_call(
        copy_kernel,
        in_specs=[anywhere] * 4,
        out_specs=[anywhere] * 4,
        out_shape=[jax.ShapeDtypeStruct((cols, PIX, inner), BF16)] * 4,
        scratch_shapes=[dma((4,))],
        compiler_params=pltpu.CompilerParams(vmem_limit_bytes=54787072),
    )(*out)
    return tuple(x.reshape(shape) for x in out)


def solution(mesh):
    blocks = P(("slide", "row"), None, None, None, None)
    return jax.shard_map(
        local,
        mesh=mesh,
        in_specs=(blocks, blocks, blocks, blocks, P("slide", None)),
        out_specs=(blocks, blocks, blocks, blocks),
        check_vma=False,
    )
```

```python
import functools

import jax
import jax.numpy as jnp
from jax import lax
from jax.experimental import pallas as pl
from jax.experimental.pallas import tpu as pltpu
from jax.sharding import PartitionSpec as P

HEAD_DIM = 64
TILE_SIDE = 8
WINDOW = 13
GRID_C = 8
PIX = TILE_SIDE * TILE_SIDE
HALF = (WINDOW - 1) // 2
REACH = HALF * TILE_SIDE
SKIP = PIX - REACH
WIDTH = 256
SUB = WIDTH // HEAD_DIM
MASKED = -1e30
F32 = jnp.float32
BF16 = jnp.bfloat16
MESH = pl.DeviceIdType.MESH


def dot(a, b, ca, cb):
    return lax.dot_general(a, b, (((ca,), (cb,)), ((), ())), preferred_element_type=F32)


def fold_rows(x):
    total = x[:PIX]
    for i in range(1, SUB):
        total = total + x[i * PIX : (i + 1) * PIX]
    return total


def kernel(
    count, nv, cols, groups,
    tissue, q_ref, k_ref, v_ref, g_ref, att_ref, dq_ref, dk_ref, dv_ref,
    q_s, g_s, rowx, vertx, bias, drow, dvert, hrow_s, hvert_s, hrow_r, hvert_r, relay_r, vert_s, vert_r, outs,
    load_sem, store_sem, side_ss, side_rs, up_ss, up_rs, edge_ss, edge_rs,
    hrow_ss, hrow_rs, hvert_ss, hvert_rs, vert_ss, vert_rs, relay_ss, relay_rs, relay_back_ss, relay_back_rs,
):
    slide, me = lax.axis_index("slide"), lax.axis_index("row")
    block = lax.rem(me + GRID_C // 2, count)
    grid_row, grid_col = lax.div(block, GRID_C), lax.rem(block, GRID_C)
    block_rows = count // GRID_C

    def at(distance):
        return (slide, lax.rem(me + distance + count, count))

    left, right = at(-1), at(1)
    if nv == 1:
        above = grid_row == 1
        deferred = above
        distance = [GRID_C]
        start = [jnp.where(above, 0, SKIP)]
        places = [(jnp.where(above, -1, 1), jnp.where(above, -HALF, TILE_SIDE))]
        seam_left = grid_col == GRID_C // 2
        seam_right = grid_col == GRID_C // 2 - 1
        seam = jnp.logical_or(seam_left, seam_right)
        across = at(jnp.where(seam_left, GRID_C - 1, GRID_C + 1))
    else:
        distance = [GRID_C, -GRID_C]
        start = [jnp.int32(SKIP), jnp.int32(0)]
        places = [(-1, -HALF), (1, TILE_SIDE)]
        seam_left = seam_right = seam = deferred = None
    start = [pl.multiple_of(x, 16) for x in start]
    seams = (seam_left, seam_right)
    if seam is not None:
        start_other = pl.multiple_of(SKIP - start[0], 16)
        rest = pl.multiple_of(jnp.where(above, REACH, 0), 16)

    def lanes(i):
        return pl.ds(pl.multiple_of(i * WIDTH, WIDTH), WIDTH)

    kv = (k_ref, v_ref)
    loads = [pltpu.make_async_copy(x, y, load_sem.at[j]) for j, (x, y) in enumerate((
        (k_ref, rowx.at[0, pl.ds(1, cols)]), (v_ref, rowx.at[1, pl.ds(1, cols)]), (q_ref, q_s), (g_ref, g_s),
    ))]

    def remote(src, dst, ss, rs, device):
        return pltpu.make_async_remote_copy(
            src_ref=src, dst_ref=dst, send_sem=ss, recv_sem=rs, device_id=device, device_id_type=MESH
        )

    def up(i, z, v):
        return remote(
            kv[z].at[:, pl.ds(start[v], REACH), lanes(i)],
            vertx.at[z, v, pl.ds(1, cols), :, lanes(i)],
            up_ss.at[i, z, v], up_rs.at[i, z, v], at(distance[v]),
        )

    def sideways(z, d, seamed=False):
        src, dst = kv[z].at[0 if d == 0 else cols - 1], rowx.at[z, cols + 1 if d == 0 else 0]
        if seamed:
            src, dst = src.at[pl.ds(rest, SKIP)], dst.at[pl.ds(rest, SKIP)]
        return remote(src, dst, side_ss.at[z, d], side_rs.at[z, d], left if d == 0 else right)

    def relay(i, z, d):
        return remote(
            vertx.at[z, 0, 1 if d == 0 else cols, :, lanes(i)],
            rowx.at[z, cols + 1 if d == 0 else 0, pl.ds(start_other, REACH), lanes(i)],
            relay_ss.at[i, z], relay_rs.at[i, z], across,
        )

    def by_seam(d, run):
        if seam is None:
            run(False)
        else:
            pl.when(seams[d])(lambda: run(True))
            pl.when(jnp.logical_not(seams[d]))(lambda: run(False))

    def edge(i, z, d):
        return remote(
            vertx.at[z, :, 1 if d == 0 else cols, :, lanes(i)], vertx.at[z, :, cols + 1 if d == 0 else 0, :, lanes(i)],
            edge_ss.at[i, z, d], edge_rs.at[i, z, d], left if d == 0 else right,
        )

    def diagonal(i, z, d):
        return remote(
            kv[z].at[0 if d == 0 else cols - 1, pl.ds(start[0], REACH), lanes(i)],
            vertx.at[z, 0, cols + 1 if d == 0 else 0, :, lanes(i)],
            edge_ss.at[i, z, d], edge_rs.at[i, z, d], across,
        )

    def row_back(i, d, seamed=False):
        rows = pl.ds(rest, SKIP) if seamed else slice(None)
        return remote(
            hrow_s.at[d, :, rows, lanes(i)], hrow_r.at[1 - d, :, rows, lanes(i)],
            hrow_ss.at[i, d], hrow_rs.at[i, d], left if d == 0 else right,
        )

    def relay_back(i, d):
        return remote(
            hrow_s.at[d, :, pl.ds(start[0], REACH), lanes(i)], relay_r.at[:, :, lanes(i)],
            relay_back_ss.at[i], relay_back_rs.at[i], across,
        )

    def vert_back(i, d):
        device = left if d == 0 else right
        if seam is not None:
            device = (slide, jnp.where(seams[d], across[1], device[1]))
        return remote(
            hvert_s.at[d, :, :, :, lanes(i)], hvert_r.at[1 - d, :, :, :, lanes(i)],
            hvert_ss.at[i, d], hvert_rs.at[i, d], device,
        )

    def down(i, v):
        return remote(
            vert_s.at[:, v, :, :, lanes(i)], vert_r.at[:, v, :, :, lanes(i)],
            vert_ss.at[i, v], vert_rs.at[i, v], at(-distance[v]),
        )

    def store(i, j):
        return pltpu.make_async_copy(
            outs.at[j, :, :, lanes(i)], (att_ref, dq_ref, dk_ref, dv_ref)[j].at[:, :, lanes(i)], store_sem.at[i, j]
        )

    barrier = pltpu.get_barrier_semaphore()
    for device in [left, right] + [at(x) for x in distance]:
        pl.semaphore_signal(barrier, inc=1, device_id=device, device_id_type=MESH)
    if seam is not None:
        @pl.when(seam)
        def _():
            pl.semaphore_signal(barrier, inc=1, device_id=across, device_id_type=MESH)
    for copy in loads:
        copy.start()
    pl.semaphore_wait(barrier, 2 + nv + (0 if seam is None else seam.astype(jnp.int32)))

    for z in range(2):
        for v in range(nv):
            up(0, z, v).start()
    for d in range(2):
        def send(seamed, d=d):
            for z in range(2):
                sideways(z, d, seamed).start()
        by_seam(d, send)
    def send_rest():
        for i in range(1, groups):
            for z in range(2):
                for v in range(nv):
                    up(i, z, v).start()
    if deferred is None:
        send_rest()
    else:
        pl.when(jnp.logical_not(deferred))(send_rest)
    if seam is not None:
        for d in range(2):
            @pl.when(seams[d])
            def _():
                for i in range(groups):
                    for z in range(2):
                        diagonal(i, z, d).start()

    query = lax.broadcasted_iota(jnp.int32, (PIX, WIDTH), 1) % PIX
    line = lax.broadcasted_iota(jnp.int32, (PIX, WIDTH), 0)
    top = 0
    for step_row, first, rows in [(0, 0, PIX)] + [(r, f, REACH) for r, f in places]:
        row_gap = first + line[:rows] // TILE_SIDE - query[:rows] // TILE_SIDE
        row = grid_row + step_row
        for step in (-1, 0, 1):
            col_gap = TILE_SIDE * step + line[:rows] % TILE_SIDE - query[:rows] % TILE_SIDE
            near = (jnp.abs(row_gap) <= HALF) & (jnp.abs(col_gap) <= HALF)
            near = jnp.where(near, 0.0, MASKED)
            for c in range(cols):
                col = grid_col * cols + c + step
                inside = (row >= 0) & (row < block_rows) & (col >= 0) & (col < GRID_C * cols)
                flag = tissue[jnp.clip(row, 0, block_rows - 1), jnp.clip(col, 0, GRID_C * cols - 1)]
                shut = jnp.where(inside & (flag > 0), 0.0, MASKED)
                bias[c, top : top + rows] = jnp.minimum(near, shut)
            top += rows
    drow[...] = jnp.zeros_like(drow)
    dvert[...] = jnp.zeros_like(dvert)

    same = (
        lax.broadcasted_iota(jnp.int32, (WIDTH, WIDTH), 0) // PIX
        == lax.broadcasted_iota(jnp.int32, (WIDTH, WIDTH), 1) // HEAD_DIM
    )
    same_low = jnp.where(same, 1.0, 0.0).astype(BF16)

    def keys_of(z, c, i):
        parts = [rowx[z, c : c + 3, :, lanes(i)].reshape(3 * PIX, WIDTH)]
        for v in range(nv):
            parts.append(vertx[z, v, c : c + 3, :, lanes(i)].reshape(3 * REACH, WIDTH))
        return jnp.concatenate(parts, axis=0)

    def attend(i):
        for c in range(cols):
            flag = tissue[grid_row, grid_col * cols + c].astype(F32)
            live = jnp.where(same, flag, 0.0)
            q = q_s[c, :, lanes(i)] * 0.125
            qbd = jnp.concatenate([q] * SUB, axis=0) * same_low
            g = g_s[c, :, lanes(i)]
            gbd = jnp.concatenate([g] * SUB, axis=0) * live.astype(BF16)
            kc, vc = keys_of(0, c, i), keys_of(1, c, i)
            s = dot(kc, qbd, 1, 1) + bias[c]
            peak = jnp.max(s, axis=0, keepdims=True)
            p = jnp.exp(s - peak)
            w = p * (1.0 / jnp.sum(p, axis=0, keepdims=True))
            w_low = w.astype(BF16)
            att_t = (dot(vc, w_low, 0, 0) * live).astype(BF16)
            outs[0, c, :, lanes(i)] = fold_rows(att_t.T)
            out_dot = jnp.sum(att_t.astype(F32) * gbd.T.astype(F32), axis=0, keepdims=True)
            probe = dot(vc, gbd, 1, 1)
            ds = (w * (probe - out_dot)).astype(BF16)
            dq = jnp.where(same, dot(ds, kc, 0, 0), 0.0)
            outs[1, c, :, lanes(i)] = (fold_rows(dq) * 0.125).astype(BF16)
            for z, term in enumerate((dot(ds, qbd, 1, 0), dot(w_low, gbd, 1, 0))):
                drow[z, c : c + 3, :, lanes(i)] += term[: 3 * PIX].reshape(3, PIX, WIDTH)
                for v in range(nv):
                    first = 3 * (PIX + v * REACH)
                    dvert[z, v, c : c + 3, :, lanes(i)] += term[first : first + 3 * REACH].reshape(3, REACH, WIDTH)

    def merge(i):
        for d in range(2):
            vert_back(i, d).wait_recv()
        if seam is not None:
            @pl.when(seam)
            def _():
                relay_back(i, 0).wait_recv()
        for z in range(2):
            for v in range(nv):
                for c in range(cols):
                    vert_s[z, v, c, :, lanes(i)] = dvert[z, v, c + 1, :, lanes(i)].astype(BF16)
        for d, c in ((0, 0), (1, cols - 1)):
            def add(seamed, d=d, c=c):
                for z in range(2):
                    for v in range(nv):
                        edge_term = relay_r[z, :, lanes(i)] if seamed else hvert_r[d, z, v, :, lanes(i)]
                        vert_s[z, v, c, :, lanes(i)] = (
                            dvert[z, v, c + 1, :, lanes(i)] + edge_term.astype(F32)
                        ).astype(BF16)
            by_seam(d, add)
        for v in range(nv):
            down(i, v).start()

    def forward(i):
        for z in range(2):
            for v in range(nv):
                up(i, z, v).wait_recv()
        for d in range(2):
            def pass_on(seamed, d=d):
                for z in range(2):
                    (relay if seamed else edge)(i, z, d).start()
            by_seam(d, pass_on)

    if deferred is not None:
        @pl.when(deferred)
        def _():
            for i in range(groups):
                forward(i)
                if i > 0:
                    for z in range(2):
                        for v in range(nv):
                            up(i, z, v).start()

    def step(i, _):
        if deferred is None:
            forward(i)
        else:
            pl.when(jnp.logical_not(deferred))(lambda: forward(i))

        @pl.when(i > 0)
        def _():
            merge(i - 1)

        @pl.when(i == 0)
        def _():
            for copy in loads:
                copy.wait()
            for d in range(2):
                def wait(seamed, d=d):
                    for z in range(2):
                        sideways(z, d, seamed).wait_recv()
                by_seam(1 - d, wait)

        for z in range(2):
            for d in range(2):
                edge(i, z, d).wait_recv()
        if seam is not None:
            for d in range(2):
                @pl.when(seams[1 - d])
                def _():
                    for z in range(2):
                        relay(i, z, d).wait_recv()
        attend(i)
        for d, tile in ((0, 0), (1, cols + 1)):
            for z in range(2):
                hrow_s[d, z, :, lanes(i)] = drow[z, tile, :, lanes(i)].astype(BF16)
                for v in range(nv):
                    hvert_s[d, z, v, :, lanes(i)] = dvert[z, v, tile, :, lanes(i)].astype(BF16)
            def give(seamed, d=d):
                if seamed:
                    relay_back(i, d).start()
                row_back(i, d, seamed).start()
            vert_back(i, d).start()
            by_seam(d, give)
        for j in range(2):
            store(i, j).start()
        return 0

    lax.fori_loop(0, groups, step, 0)
    merge(groups - 1)

    def gather(i, _):
        for d, c in ((1, 0), (0, cols - 1)):
            def add(seamed, d=d, c=c):
                row_back(i, d, seamed).wait_recv()
                rows = pl.ds(rest, SKIP) if seamed else slice(None)
                for z in range(2):
                    drow[z, c + 1, rows, lanes(i)] += hrow_r[1 - d, z, rows, lanes(i)].astype(F32)
                    if seamed:
                        drow[z, c + 1, pl.ds(start[0], REACH), lanes(i)] += hvert_r[1 - d, z, 0, :, lanes(i)].astype(F32)
            by_seam(1 - d, add)
        return 0

    def finish(i, _):
        for v in range(nv):
            down(i, v).wait_recv()
        for z in range(2):
            for c in range(cols):
                for v in range(nv):
                    drow[z, c + 1, pl.ds(start[v], REACH), lanes(i)] += vert_r[z, v, c, :, lanes(i)].astype(F32)
            outs[2 + z, :, :, lanes(i)] = drow[z, 1 : cols + 1, :, lanes(i)].astype(BF16)
            store(i, 2 + z).start()
        return 0

    lax.fori_loop(0, groups, gather, 0)
    lax.fori_loop(0, groups, finish, 0)

    def drain(i, _):
        for z in range(2):
            for v in range(nv):
                up(i, z, v).wait_send()
            for d in range(2):
                edge(i, z, d).wait_send()
        if seam is not None:
            for d in range(2):
                @pl.when(seams[d])
                def _():
                    for z in range(2):
                        relay(i, z, d).wait_send()
        for d in range(2):
            def sent(seamed, d=d):
                if seamed:
                    relay_back(i, d).wait_send()
                row_back(i, d, seamed).wait_send()
            vert_back(i, d).wait_send()
            by_seam(d, sent)
        for v in range(nv):
            down(i, v).wait_send()
        for j in range(4):
            store(i, j).wait()
        return 0

    for d in range(2):
        def sent(seamed, d=d):
            for z in range(2):
                sideways(z, d, seamed).wait_send()
        by_seam(d, sent)
    lax.fori_loop(0, groups, drain, 0)


def copy_kernel(*refs):
    sem = refs[-1]
    copies = [pltpu.make_async_copy(refs[j], refs[4 + j], sem.at[j]) for j in range(4)]
    for copy in copies:
        copy.start()
    for copy in copies:
        copy.wait()


def local(query_states, key_states, value_states, grad_output, tissue_map):
    shape = query_states.shape
    cols, inner = shape[2], shape[4]
    q, k, v, g = (x.reshape(cols, PIX, inner) for x in (query_states, key_states, value_states, grad_output))
    count = lax.axis_size("row")
    nv = 1 if count // GRID_C == 2 else 2
    groups = inner // WIDTH
    seen = 3 * (PIX + nv * REACH)
    dma = pltpu.SemaphoreType.DMA
    anywhere = pl.BlockSpec(memory_space=pl.ANY)
    out = pl.pallas_call(
        functools.partial(kernel, count, nv, cols, groups),
        in_specs=[pl.BlockSpec(memory_space=pltpu.SMEM)] + [anywhere] * 4,
        out_specs=[anywhere] * 4,
        out_shape=[jax.ShapeDtypeStruct((cols, PIX, inner), BF16)] * 4,
        scratch_shapes=[
            pltpu.VMEM((cols, PIX, inner), BF16),
            pltpu.VMEM((cols, PIX, inner), BF16),
            pltpu.VMEM((2, cols + 2, PIX, inner), BF16),
            pltpu.VMEM((2, nv, cols + 2, REACH, inner), BF16),
            pltpu.VMEM((cols, seen, WIDTH), F32),
            pltpu.VMEM((2, cols + 2, PIX, inner), F32),
            pltpu.VMEM((2, nv, cols + 2, REACH, inner), F32),
            pltpu.VMEM((2, 2, PIX, inner), BF16),
            pltpu.VMEM((2, 2, nv, REACH, inner), BF16),
            pltpu.VMEM((2, 2, PIX, inner), BF16),
            pltpu.VMEM((2, 2, nv, REACH, inner), BF16),
            pltpu.VMEM((2, REACH, inner), BF16),
            pltpu.VMEM((2, nv, cols, REACH, inner), BF16),
            pltpu.VMEM((2, nv, cols, REACH, inner), BF16),
            pltpu.VMEM((4, cols, PIX, inner), BF16),
            dma((4,)), dma((groups, 4)),
            dma((2, 2)), dma((2, 2)),
            dma((groups, 2, nv)), dma((groups, 2, nv)),
            dma((groups, 2, 2)), dma((groups, 2, 2)),
            dma((groups, 2)), dma((groups, 2)),
            dma((groups, 2)), dma((groups, 2)),
            dma((groups, nv)), dma((groups, nv)),
            dma((groups, 2)), dma((groups, 2)), dma((groups,)), dma((groups,)),
        ],
        compiler_params=pltpu.CompilerParams(
            collective_id=0, has_side_effects=True, vmem_limit_bytes=40 << 20
        ),
        cost_estimate=pl.CostEstimate(
            flops=groups * cols * seen * WIDTH * WIDTH * 2 * 6,
            bytes_accessed=8 << 20,
            transcendentals=groups * cols * seen * WIDTH,
        ),
    )(*(pltpu.with_memory_space_constraint(x, pltpu.HBM) for x in (tissue_map, q, k, v, g)))
    out = pl.pallas_call(
        copy_kernel,
        in_specs=[anywhere] * 4,
        out_specs=[anywhere] * 4,
        out_shape=[jax.ShapeDtypeStruct((cols, PIX, inner), BF16)] * 4,
        scratch_shapes=[dma((4,))],
        compiler_params=pltpu.CompilerParams(vmem_limit_bytes=40 << 20),
    )(*out)
    return tuple(x.reshape(shape) for x in out)


def solution(mesh):
    blocks = P(("slide", "row"), None, None, None, None)
    return jax.shard_map(
        local,
        mesh=mesh,
        in_specs=(blocks, blocks, blocks, blocks, P("slide", None)),
        out_specs=(blocks, blocks, blocks, blocks),
        check_vma=False,
    )
```

```python
import functools

import jax
import jax.numpy as jnp
from jax import lax
from jax.experimental import pallas as pl
from jax.experimental.pallas import tpu as pltpu
from jax.sharding import PartitionSpec as P

HEAD_DIM = 64
TILE_SIDE = 8
WINDOW = 13
GRID_C = 8
PIX = TILE_SIDE * TILE_SIDE
HALF = (WINDOW - 1) // 2
REACH = HALF * TILE_SIDE
SKIP = PIX - REACH
WIDTH = 256
SUB = WIDTH // HEAD_DIM
MASKED = -1e30
F32 = jnp.float32
BF16 = jnp.bfloat16
MESH = pl.DeviceIdType.MESH


def dot(a, b, ca, cb):
    return lax.dot_general(a, b, (((ca,), (cb,)), ((), ())), preferred_element_type=F32)


def fold_rows(x):
    total = x[:PIX]
    for i in range(1, SUB):
        total = total + x[i * PIX : (i + 1) * PIX]
    return total


def kernel(
    count, nv, cols, groups,
    tissue, q_ref, k_ref, v_ref, g_ref, att_ref, dq_ref, dk_ref, dv_ref,
    q_s, g_s, rowx, vertx, bias, drow, dvert, hrow_s, hvert_s, hrow_r, hvert_r, relay_r, vert_s, vert_r, outs,
    load_sem, store_sem, side_ss, side_rs, up_ss, up_rs, edge_ss, edge_rs,
    hrow_ss, hrow_rs, hvert_ss, hvert_rs, vert_ss, vert_rs, relay_ss, relay_rs, relay_back_ss, relay_back_rs,
):
    slide, me = lax.axis_index("slide"), lax.axis_index("row")
    block = lax.rem(me + GRID_C // 2, count)
    grid_row, grid_col = lax.div(block, GRID_C), lax.rem(block, GRID_C)
    block_rows = count // GRID_C

    def at(distance):
        return (slide, lax.rem(me + distance + count, count))

    left, right = at(-1), at(1)
    if nv == 1:
        above = grid_row == 1
        hasty = above
        distance = [GRID_C]
        start = [jnp.where(above, 0, SKIP)]
        places = [(jnp.where(above, -1, 1), jnp.where(above, -HALF, TILE_SIDE))]
        seam_left = grid_col == GRID_C // 2
        seam_right = grid_col == GRID_C // 2 - 1
        seam = jnp.logical_or(seam_left, seam_right)
        across = at(jnp.where(seam_left, GRID_C - 1, GRID_C + 1))
    else:
        distance = [GRID_C, -GRID_C]
        start = [jnp.int32(SKIP), jnp.int32(0)]
        places = [(-1, -HALF), (1, TILE_SIDE)]
        seam_left = seam_right = seam = hasty = None
    start = [pl.multiple_of(x, 16) for x in start]
    seams = (seam_left, seam_right)
    walls = (grid_col == 0, grid_col == GRID_C - 1)
    if seam is not None:
        start_other = pl.multiple_of(SKIP - start[0], 16)
        rest = pl.multiple_of(jnp.where(above, REACH, 0), 16)

    def lanes(i):
        return pl.ds(pl.multiple_of(i * WIDTH, WIDTH), WIDTH)

    kv = (k_ref, v_ref)
    loads = [pltpu.make_async_copy(x, y, load_sem.at[j]) for j, (x, y) in enumerate((
        (k_ref, rowx.at[0, pl.ds(1, cols)]), (v_ref, rowx.at[1, pl.ds(1, cols)]), (q_ref, q_s), (g_ref, g_s),
    ))]

    def remote(src, dst, ss, rs, device):
        return pltpu.make_async_remote_copy(
            src_ref=src, dst_ref=dst, send_sem=ss, recv_sem=rs, device_id=device, device_id_type=MESH
        )

    def up(i, z, v):
        return remote(
            kv[z].at[:, pl.ds(start[v], REACH), lanes(i)],
            vertx.at[z, v, pl.ds(1, cols), :, lanes(i)],
            up_ss.at[i, z, v], up_rs.at[i, z, v], at(distance[v]),
        )

    def sideways(z, d, seamed=False):
        src, dst = kv[z].at[0 if d == 0 else cols - 1], rowx.at[z, cols + 1 if d == 0 else 0]
        if seamed:
            src, dst = src.at[pl.ds(rest, SKIP)], dst.at[pl.ds(rest, SKIP)]
        return remote(src, dst, side_ss.at[z, d], side_rs.at[z, d], left if d == 0 else right)

    def relay(i, z, d):
        return remote(
            vertx.at[z, 0, 1 if d == 0 else cols, :, lanes(i)],
            rowx.at[z, cols + 1 if d == 0 else 0, pl.ds(start_other, REACH), lanes(i)],
            relay_ss.at[i, z], relay_rs.at[i, z], across,
        )

    def by_side(d, run):
        if seam is None:
            pl.when(jnp.logical_not(walls[d]))(lambda: run(False))
        else:
            pl.when(seams[d])(lambda: run(True))
            pl.when(jnp.logical_not(jnp.logical_or(seams[d], walls[d])))(lambda: run(False))

    def beside(d, run):
        pl.when(jnp.logical_not(walls[d]))(run)

    def edge(i, z, d):
        return remote(
            vertx.at[z, :, 1 if d == 0 else cols, :, lanes(i)], vertx.at[z, :, cols + 1 if d == 0 else 0, :, lanes(i)],
            edge_ss.at[i, z, d], edge_rs.at[i, z, d], left if d == 0 else right,
        )

    def diagonal(i, z, d):
        return remote(
            kv[z].at[0 if d == 0 else cols - 1, pl.ds(start[0], REACH), lanes(i)],
            vertx.at[z, 0, cols + 1 if d == 0 else 0, :, lanes(i)],
            edge_ss.at[i, z, d], edge_rs.at[i, z, d], across,
        )

    def row_back(i, d, seamed=False):
        rows = pl.ds(rest, SKIP) if seamed else slice(None)
        return remote(
            hrow_s.at[d, :, rows, lanes(i)], hrow_r.at[1 - d, :, rows, lanes(i)],
            hrow_ss.at[i, d], hrow_rs.at[i, d], left if d == 0 else right,
        )

    def relay_back(i, d):
        return remote(
            hrow_s.at[d, :, pl.ds(start[0], REACH), lanes(i)], relay_r.at[:, :, lanes(i)],
            relay_back_ss.at[i], relay_back_rs.at[i], across,
        )

    def vert_back(i, d):
        device = left if d == 0 else right
        if seam is not None:
            device = (slide, jnp.where(seams[d], across[1], device[1]))
        return remote(
            hvert_s.at[d, :, :, :, lanes(i)], hvert_r.at[1 - d, :, :, :, lanes(i)],
            hvert_ss.at[i, d], hvert_rs.at[i, d], device,
        )

    def down(i, v):
        return remote(
            vert_s.at[:, v, :, :, lanes(i)], vert_r.at[:, v, :, :, lanes(i)],
            vert_ss.at[i, v], vert_rs.at[i, v], at(-distance[v]),
        )

    def store(i, j):
        return pltpu.make_async_copy(
            outs.at[j, :, :, lanes(i)], (att_ref, dq_ref, dk_ref, dv_ref)[j].at[:, :, lanes(i)], store_sem.at[i, j]
        )

    barrier = pltpu.get_barrier_semaphore()
    def greet(device):
        pl.semaphore_signal(barrier, inc=1, device_id=device, device_id_type=MESH)
    for x in distance:
        greet(at(x))
    if seam is not None:
        pl.when(seam)(lambda: greet(across))
    for d in range(2):
        beside(d, lambda: greet((left, right)[d]))
    for copy in loads:
        copy.start()
    peers = 2 + nv - jnp.logical_or(*walls).astype(jnp.int32)
    if seam is not None:
        peers = peers + seam.astype(jnp.int32)
    pl.semaphore_wait(barrier, peers)

    for z in range(2):
        for v in range(nv):
            up(0, z, v).start()
    for d in range(2):
        def send(seamed, d=d):
            for z in range(2):
                sideways(z, d, seamed).start()
        by_side(d, send)
    if seam is not None:
        for d in range(2):
            @pl.when(seams[d])
            def _():
                for i in range(groups):
                    for z in range(2):
                        diagonal(i, z, d).start()

    query = lax.broadcasted_iota(jnp.int32, (PIX, WIDTH), 1) % PIX
    line = lax.broadcasted_iota(jnp.int32, (PIX, WIDTH), 0)
    top = 0
    for step_row, first, rows in [(0, 0, PIX)] + [(r, f, REACH) for r, f in places]:
        row_gap = first + line[:rows] // TILE_SIDE - query[:rows] // TILE_SIDE
        row = grid_row + step_row
        for step in (-1, 0, 1):
            col_gap = TILE_SIDE * step + line[:rows] % TILE_SIDE - query[:rows] % TILE_SIDE
            near = (jnp.abs(row_gap) <= HALF) & (jnp.abs(col_gap) <= HALF)
            near = jnp.where(near, 0.0, MASKED)
            for c in range(cols):
                col = grid_col * cols + c + step
                inside = (row >= 0) & (row < block_rows) & (col >= 0) & (col < GRID_C * cols)
                flag = tissue[jnp.clip(row, 0, block_rows - 1), jnp.clip(col, 0, GRID_C * cols - 1)]
                shut = jnp.where(inside & (flag > 0), 0.0, MASKED)
                bias[c, top : top + rows] = jnp.minimum(near, shut)
            top += rows
    for d, tile in ((0, 0), (1, cols + 1)):
        @pl.when(walls[d])
        def _():
            rowx[:, tile] = jnp.zeros((2, PIX, rowx.shape[-1]), BF16)
            vertx[:, :, tile] = jnp.zeros((2, nv, REACH, rowx.shape[-1]), BF16)
    drow[...] = jnp.zeros_like(drow)
    dvert[...] = jnp.zeros_like(dvert)

    same = (
        lax.broadcasted_iota(jnp.int32, (WIDTH, WIDTH), 0) // PIX
        == lax.broadcasted_iota(jnp.int32, (WIDTH, WIDTH), 1) // HEAD_DIM
    )
    same_low = jnp.where(same, 1.0, 0.0).astype(BF16)

    def keys_of(z, c, i):
        parts = [rowx[z, c : c + 3, :, lanes(i)].reshape(3 * PIX, WIDTH)]
        for v in range(nv):
            parts.append(vertx[z, v, c : c + 3, :, lanes(i)].reshape(3 * REACH, WIDTH))
        return jnp.concatenate(parts, axis=0)

    def attend(i):
        for c in range(cols):
            flag = tissue[grid_row, grid_col * cols + c].astype(F32)
            live = jnp.where(same, flag, 0.0)
            q = q_s[c, :, lanes(i)] * 0.125
            qbd = jnp.concatenate([q] * SUB, axis=0) * same_low
            g = g_s[c, :, lanes(i)]
            gbd = jnp.concatenate([g] * SUB, axis=0) * live.astype(BF16)
            kc, vc = keys_of(0, c, i), keys_of(1, c, i)
            s = dot(kc, qbd, 1, 1) + bias[c]
            peak = jnp.max(s, axis=0, keepdims=True)
            p = jnp.exp(s - peak)
            w = p * (1.0 / jnp.sum(p, axis=0, keepdims=True))
            w_low = w.astype(BF16)
            att_t = (dot(vc, w_low, 0, 0) * live).astype(BF16)
            outs[0, c, :, lanes(i)] = fold_rows(att_t.T)
            out_dot = jnp.sum(att_t.astype(F32) * gbd.T.astype(F32), axis=0, keepdims=True)
            probe = dot(vc, gbd, 1, 1)
            ds = (w * (probe - out_dot)).astype(BF16)
            dq = jnp.where(same, dot(ds, kc, 0, 0), 0.0)
            outs[1, c, :, lanes(i)] = (fold_rows(dq) * 0.125).astype(BF16)
            for z, term in enumerate((dot(ds, qbd, 1, 0), dot(w_low, gbd, 1, 0))):
                drow[z, c : c + 3, :, lanes(i)] += term[: 3 * PIX].reshape(3, PIX, WIDTH)
                for v in range(nv):
                    first = 3 * (PIX + v * REACH)
                    dvert[z, v, c : c + 3, :, lanes(i)] += term[first : first + 3 * REACH].reshape(3, REACH, WIDTH)

    def merge(i):
        for d in range(2):
            beside(1 - d, lambda: vert_back(i, d).wait_recv())
        if seam is not None:
            @pl.when(seam)
            def _():
                relay_back(i, 0).wait_recv()
        for z in range(2):
            for v in range(nv):
                for c in range(cols):
                    vert_s[z, v, c, :, lanes(i)] = dvert[z, v, c + 1, :, lanes(i)].astype(BF16)
        for d, c in ((0, 0), (1, cols - 1)):
            def add(seamed, d=d, c=c):
                for z in range(2):
                    for v in range(nv):
                        edge_term = relay_r[z, :, lanes(i)] if seamed else hvert_r[d, z, v, :, lanes(i)]
                        vert_s[z, v, c, :, lanes(i)] = (
                            dvert[z, v, c + 1, :, lanes(i)] + edge_term.astype(F32)
                        ).astype(BF16)
            by_side(d, add)

    def send_down(i):
        for v in range(nv):
            down(i, v).start()

    def forward(i):
        for z in range(2):
            for v in range(nv):
                up(i, z, v).wait_recv()
        for d in range(2):
            def pass_on(seamed, d=d):
                for z in range(2):
                    (relay if seamed else edge)(i, z, d).start()
            by_side(d, pass_on)

    def step(i, _):
        forward(i)

        @pl.when(i + 1 < groups)
        def _():
            for z in range(2):
                for v in range(nv):
                    up(i + 1, z, v).start()

        @pl.when(i > 0)
        def _():
            merge(i - 1)
            if hasty is not None:
                pl.when(hasty)(lambda: send_down(i - 1))

        @pl.when(i == 0)
        def _():
            for copy in loads:
                copy.wait()
            for d in range(2):
                def wait(seamed, d=d):
                    for z in range(2):
                        sideways(z, d, seamed).wait_recv()
                by_side(1 - d, wait)

        for d in range(2):
            @functools.partial(beside, 1 - d)
            def _():
                for z in range(2):
                    edge(i, z, d).wait_recv()
        if seam is not None:
            for d in range(2):
                @pl.when(seams[1 - d])
                def _():
                    for z in range(2):
                        relay(i, z, d).wait_recv()
        attend(i)
        for d, tile in ((0, 0), (1, cols + 1)):
            for z in range(2):
                hrow_s[d, z, :, lanes(i)] = drow[z, tile, :, lanes(i)].astype(BF16)
                for v in range(nv):
                    hvert_s[d, z, v, :, lanes(i)] = dvert[z, v, tile, :, lanes(i)].astype(BF16)
            def give(seamed, d=d):
                if seamed:
                    relay_back(i, d).start()
                row_back(i, d, seamed).start()
                vert_back(i, d).start()
            by_side(d, give)

        late = i > 0 if hasty is None else jnp.logical_and(i > 0, jnp.logical_not(hasty))
        pl.when(late)(lambda: send_down(i - 1))
        for j in range(2):
            store(i, j).start()
        return 0

    lax.fori_loop(0, groups, step, 0)
    merge(groups - 1)
    send_down(groups - 1)

    def gather(i, _):
        for d, c in ((1, 0), (0, cols - 1)):
            def add(seamed, d=d, c=c):
                row_back(i, d, seamed).wait_recv()
                rows = pl.ds(rest, SKIP) if seamed else slice(None)
                for z in range(2):
                    drow[z, c + 1, rows, lanes(i)] += hrow_r[1 - d, z, rows, lanes(i)].astype(F32)
                    if seamed:
                        drow[z, c + 1, pl.ds(start[0], REACH), lanes(i)] += hvert_r[1 - d, z, 0, :, lanes(i)].astype(F32)
            by_side(1 - d, add)
        return 0

    def finish(i, _):
        for v in range(nv):
            down(i, v).wait_recv()
        for z in range(2):
            for c in range(cols):
                for v in range(nv):
                    drow[z, c + 1, pl.ds(start[v], REACH), lanes(i)] += vert_r[z, v, c, :, lanes(i)].astype(F32)
            outs[2 + z, :, :, lanes(i)] = drow[z, 1 : cols + 1, :, lanes(i)].astype(BF16)
            store(i, 2 + z).start()
        return 0

    lax.fori_loop(0, groups, gather, 0)
    lax.fori_loop(0, groups, finish, 0)

    def drain(i, _):
        for z in range(2):
            for v in range(nv):
                up(i, z, v).wait_send()
            for d in range(2):
                beside(d, lambda: edge(i, z, d).wait_send())
        if seam is not None:
            for d in range(2):
                @pl.when(seams[d])
                def _():
                    for z in range(2):
                        relay(i, z, d).wait_send()
        for d in range(2):
            def sent(seamed, d=d):
                if seamed:
                    relay_back(i, d).wait_send()
                row_back(i, d, seamed).wait_send()
                vert_back(i, d).wait_send()
            by_side(d, sent)
        for v in range(nv):
            down(i, v).wait_send()
        for j in range(4):
            store(i, j).wait()
        return 0

    for d in range(2):
        def sent(seamed, d=d):
            for z in range(2):
                sideways(z, d, seamed).wait_send()
        by_side(d, sent)
    lax.fori_loop(0, groups, drain, 0)


def copy_kernel(*refs):
    sem = refs[-1]
    copies = [pltpu.make_async_copy(refs[j], refs[4 + j], sem.at[j]) for j in range(4)]
    for copy in copies:
        copy.start()
    for copy in copies:
        copy.wait()


def local(query_states, key_states, value_states, grad_output, tissue_map):
    shape = query_states.shape
    cols, inner = shape[2], shape[4]
    q, k, v, g = (x.reshape(cols, PIX, inner) for x in (query_states, key_states, value_states, grad_output))
    count = lax.axis_size("row")
    nv = 1 if count // GRID_C == 2 else 2
    groups = inner // WIDTH
    seen = 3 * (PIX + nv * REACH)
    dma = pltpu.SemaphoreType.DMA
    anywhere = pl.BlockSpec(memory_space=pl.ANY)
    out = pl.pallas_call(
        functools.partial(kernel, count, nv, cols, groups),
        in_specs=[pl.BlockSpec(memory_space=pltpu.SMEM)] + [anywhere] * 4,
        out_specs=[anywhere] * 4,
        out_shape=[jax.ShapeDtypeStruct((cols, PIX, inner), BF16)] * 4,
        scratch_shapes=[
            pltpu.VMEM((cols, PIX, inner), BF16),
            pltpu.VMEM((cols, PIX, inner), BF16),
            pltpu.VMEM((2, cols + 2, PIX, inner), BF16),
            pltpu.VMEM((2, nv, cols + 2, REACH, inner), BF16),
            pltpu.VMEM((cols, seen, WIDTH), F32),
            pltpu.VMEM((2, cols + 2, PIX, inner), F32),
            pltpu.VMEM((2, nv, cols + 2, REACH, inner), F32),
            pltpu.VMEM((2, 2, PIX, inner), BF16),
            pltpu.VMEM((2, 2, nv, REACH, inner), BF16),
            pltpu.VMEM((2, 2, PIX, inner), BF16),
            pltpu.VMEM((2, 2, nv, REACH, inner), BF16),
            pltpu.VMEM((2, REACH, inner), BF16),
            pltpu.VMEM((2, nv, cols, REACH, inner), BF16),
            pltpu.VMEM((2, nv, cols, REACH, inner), BF16),
            pltpu.VMEM((4, cols, PIX, inner), BF16),
            dma((4,)), dma((groups, 4)),
            dma((2, 2)), dma((2, 2)),
            dma((groups, 2, nv)), dma((groups, 2, nv)),
            dma((groups, 2, 2)), dma((groups, 2, 2)),
            dma((groups, 2)), dma((groups, 2)),
            dma((groups, 2)), dma((groups, 2)),
            dma((groups, nv)), dma((groups, nv)),
            dma((groups, 2)), dma((groups, 2)), dma((groups,)), dma((groups,)),
        ],
        compiler_params=pltpu.CompilerParams(
            collective_id=0, has_side_effects=True, vmem_limit_bytes=40 << 20
        ),
        cost_estimate=pl.CostEstimate(
            flops=groups * cols * seen * WIDTH * WIDTH * 2 * 6,
            bytes_accessed=8 << 20,
            transcendentals=groups * cols * seen * WIDTH,
        ),
    )(*(pltpu.with_memory_space_constraint(x, pltpu.HBM) for x in (tissue_map, q, k, v, g)))
    out = pl.pallas_call(
        copy_kernel,
        in_specs=[anywhere] * 4,
        out_specs=[anywhere] * 4,
        out_shape=[jax.ShapeDtypeStruct((cols, PIX, inner), BF16)] * 4,
        scratch_shapes=[dma((4,))],
        compiler_params=pltpu.CompilerParams(vmem_limit_bytes=40 << 20),
    )(*out)
    return tuple(x.reshape(shape) for x in out)


def solution(mesh):
    blocks = P(("slide", "row"), None, None, None, None)
    return jax.shard_map(
        local,
        mesh=mesh,
        in_specs=(blocks, blocks, blocks, blocks, P("slide", None)),
        out_specs=(blocks, blocks, blocks, blocks),
        check_vma=False,
    )
```

```python
import functools

import jax
import jax.numpy as jnp
from jax import lax
from jax.experimental import pallas as pl
from jax.experimental.pallas import tpu as pltpu
from jax.sharding import PartitionSpec as P

HEAD_DIM = 64
TILE_SIDE = 8
WINDOW = 13
GRID_C = 8
PIX = TILE_SIDE * TILE_SIDE
HALF = (WINDOW - 1) // 2
REACH = HALF * TILE_SIDE
SKIP = PIX - REACH
WIDTH = 256
SUB = WIDTH // HEAD_DIM
MASKED = -1e30
F32 = jnp.float32
BF16 = jnp.bfloat16
MESH = pl.DeviceIdType.MESH


def dot(a, b, ca, cb):
    return lax.dot_general(a, b, (((ca,), (cb,)), ((), ())), preferred_element_type=F32)


def fold_rows(x):
    total = x[:PIX]
    for i in range(1, SUB):
        total = total + x[i * PIX : (i + 1) * PIX]
    return total


def kernel(
    count, nv, cols, groups,
    tissue, q_ref, k_ref, v_ref, g_ref, att_ref, dq_ref, dk_ref, dv_ref,
    q_s, g_s, rowx, vertx, bias, drow, dvert, hrow_s, hvert_s, hrow_r, hvert_r, relay_r, vert_s, vert_r, outs,
    load_sem, store_sem, side_ss, side_rs, up_ss, up_rs, edge_ss, edge_rs,
    hrow_ss, hrow_rs, hvert_ss, hvert_rs, vert_ss, vert_rs, relay_ss, relay_rs, relay_back_ss, relay_back_rs,
):
    slide, me = lax.axis_index("slide"), lax.axis_index("row")
    block = lax.rem(me + GRID_C // 2, count)
    grid_row, grid_col = lax.div(block, GRID_C), lax.rem(block, GRID_C)
    block_rows = count // GRID_C

    def at(distance):
        return (slide, lax.rem(me + distance + count, count))

    left, right = at(-1), at(1)
    if nv == 1:
        above = grid_row == 1
        hasty = above
        distance = [GRID_C]
        start = [jnp.where(above, 0, SKIP)]
        places = [(jnp.where(above, -1, 1), jnp.where(above, -HALF, TILE_SIDE))]
        seam_left = grid_col == GRID_C // 2
        seam_right = grid_col == GRID_C // 2 - 1
        seam = jnp.logical_or(seam_left, seam_right)
        across = at(jnp.where(seam_left, GRID_C - 1, GRID_C + 1))
    else:
        distance = [GRID_C, -GRID_C]
        start = [jnp.int32(SKIP), jnp.int32(0)]
        places = [(-1, -HALF), (1, TILE_SIDE)]
        seam_left = seam_right = seam = hasty = None
    start = [pl.multiple_of(x, 16) for x in start]
    seams = (seam_left, seam_right)
    walls = (grid_col == 0, grid_col == GRID_C - 1)
    if seam is not None:
        start_other = pl.multiple_of(SKIP - start[0], 16)
        rest = pl.multiple_of(jnp.where(above, REACH, 0), 16)

    def lanes(i):
        return pl.ds(pl.multiple_of(i * WIDTH, WIDTH), WIDTH)

    kv = (k_ref, v_ref)
    loads = [pltpu.make_async_copy(x, y, load_sem.at[j]) for j, (x, y) in enumerate((
        (k_ref, rowx.at[0, pl.ds(1, cols)]), (v_ref, rowx.at[1, pl.ds(1, cols)]), (q_ref, q_s), (g_ref, g_s),
    ))]

    def remote(src, dst, ss, rs, device):
        return pltpu.make_async_remote_copy(
            src_ref=src, dst_ref=dst, send_sem=ss, recv_sem=rs, device_id=device, device_id_type=MESH
        )

    def up(i, z, v):
        return remote(
            kv[z].at[:, pl.ds(start[v], REACH), lanes(i)],
            vertx.at[z, v, pl.ds(1, cols), :, lanes(i)],
            up_ss.at[i, z, v], up_rs.at[i, z, v], at(distance[v]),
        )

    def sideways(z, d, seamed=False):
        src, dst = kv[z].at[0 if d == 0 else cols - 1], rowx.at[z, cols + 1 if d == 0 else 0]
        if seamed:
            src, dst = src.at[pl.ds(rest, SKIP)], dst.at[pl.ds(rest, SKIP)]
        return remote(src, dst, side_ss.at[z, d], side_rs.at[z, d], left if d == 0 else right)

    def relay(i, z, d):
        return remote(
            vertx.at[z, 0, 1 if d == 0 else cols, :, lanes(i)],
            rowx.at[z, cols + 1 if d == 0 else 0, pl.ds(start_other, REACH), lanes(i)],
            relay_ss.at[i, z], relay_rs.at[i, z], across,
        )

    def by_side(d, run):
        if seam is None:
            pl.when(jnp.logical_not(walls[d]))(lambda: run(False))
        else:
            pl.when(seams[d])(lambda: run(True))
            pl.when(jnp.logical_not(jnp.logical_or(seams[d], walls[d])))(lambda: run(False))

    def beside(d, run):
        pl.when(jnp.logical_not(walls[d]))(run)

    def edge(i, z, d):
        return remote(
            vertx.at[z, :, 1 if d == 0 else cols, :, lanes(i)], vertx.at[z, :, cols + 1 if d == 0 else 0, :, lanes(i)],
            edge_ss.at[i, z, d], edge_rs.at[i, z, d], left if d == 0 else right,
        )

    def diagonal(i, z, d):
        return remote(
            kv[z].at[0 if d == 0 else cols - 1, pl.ds(start[0], REACH), lanes(i)],
            vertx.at[z, 0, cols + 1 if d == 0 else 0, :, lanes(i)],
            edge_ss.at[i, z, d], edge_rs.at[i, z, d], across,
        )

    def row_back(i, d, seamed=False):
        rows = pl.ds(rest, SKIP) if seamed else slice(None)
        return remote(
            hrow_s.at[d, :, rows, lanes(i)], hrow_r.at[1 - d, :, rows, lanes(i)],
            hrow_ss.at[i, d], hrow_rs.at[i, d], left if d == 0 else right,
        )

    def relay_back(i, d):
        return remote(
            hrow_s.at[d, :, pl.ds(start[0], REACH), lanes(i)], relay_r.at[:, :, lanes(i)],
            relay_back_ss.at[i], relay_back_rs.at[i], across,
        )

    def vert_back(i, d):
        device = left if d == 0 else right
        if seam is not None:
            device = (slide, jnp.where(seams[d], across[1], device[1]))
        return remote(
            hvert_s.at[d, :, :, :, lanes(i)], hvert_r.at[1 - d, :, :, :, lanes(i)],
            hvert_ss.at[i, d], hvert_rs.at[i, d], device,
        )

    def down(i, z, v):
        return remote(
            vert_s.at[z, v, :, :, lanes(i)], vert_r.at[z, v, :, :, lanes(i)],
            vert_ss.at[i, z, v], vert_rs.at[i, z, v], at(-distance[v]),
        )

    def store(i, j):
        return pltpu.make_async_copy(
            outs.at[j, :, :, lanes(i)], (att_ref, dq_ref, dk_ref, dv_ref)[j].at[:, :, lanes(i)], store_sem.at[i, j]
        )

    barrier = pltpu.get_barrier_semaphore()
    def greet(device):
        pl.semaphore_signal(barrier, inc=1, device_id=device, device_id_type=MESH)
    for x in distance:
        greet(at(x))
    if seam is not None:
        pl.when(seam)(lambda: greet(across))
    for d in range(2):
        beside(d, lambda: greet((left, right)[d]))
    for copy in loads:
        copy.start()
    peers = 2 + nv - jnp.logical_or(*walls).astype(jnp.int32)
    if seam is not None:
        peers = peers + seam.astype(jnp.int32)
    pl.semaphore_wait(barrier, peers)

    for z in range(2):
        for v in range(nv):
            up(0, z, v).start()
    for d in range(2):
        def send(seamed, d=d):
            for z in range(2):
                sideways(z, d, seamed).start()
        by_side(d, send)
    if seam is not None:
        for d in range(2):
            @pl.when(seams[d])
            def _():
                for i in range(groups):
                    for z in range(2):
                        diagonal(i, z, d).start()

    query = lax.broadcasted_iota(jnp.int32, (PIX, WIDTH), 1) % PIX
    line = lax.broadcasted_iota(jnp.int32, (PIX, WIDTH), 0)
    top = 0
    for step_row, first, rows in [(0, 0, PIX)] + [(r, f, REACH) for r, f in places]:
        row_gap = first + line[:rows] // TILE_SIDE - query[:rows] // TILE_SIDE
        row = grid_row + step_row
        for step in (-1, 0, 1):
            col_gap = TILE_SIDE * step + line[:rows] % TILE_SIDE - query[:rows] % TILE_SIDE
            near = (jnp.abs(row_gap) <= HALF) & (jnp.abs(col_gap) <= HALF)
            near = jnp.where(near, 0.0, MASKED)
            for c in range(cols):
                col = grid_col * cols + c + step
                inside = (row >= 0) & (row < block_rows) & (col >= 0) & (col < GRID_C * cols)
                flag = tissue[jnp.clip(row, 0, block_rows - 1), jnp.clip(col, 0, GRID_C * cols - 1)]
                shut = jnp.where(inside & (flag > 0), 0.0, MASKED)
                bias[c, top : top + rows] = jnp.minimum(near, shut)
            top += rows
    for d, tile in ((0, 0), (1, cols + 1)):
        @pl.when(walls[d])
        def _():
            rowx[:, tile] = jnp.zeros((2, PIX, rowx.shape[-1]), BF16)
            vertx[:, :, tile] = jnp.zeros((2, nv, REACH, rowx.shape[-1]), BF16)
    drow[...] = jnp.zeros_like(drow)
    dvert[...] = jnp.zeros_like(dvert)

    same = (
        lax.broadcasted_iota(jnp.int32, (WIDTH, WIDTH), 0) // PIX
        == lax.broadcasted_iota(jnp.int32, (WIDTH, WIDTH), 1) // HEAD_DIM
    )
    same_low = jnp.where(same, 1.0, 0.0).astype(BF16)

    def keys_of(z, c, i):
        parts = [rowx[z, c : c + 3, :, lanes(i)].reshape(3 * PIX, WIDTH)]
        for v in range(nv):
            parts.append(vertx[z, v, c : c + 3, :, lanes(i)].reshape(3 * REACH, WIDTH))
        return jnp.concatenate(parts, axis=0)

    def attend(i, columns):
        for c in columns:
            flag = tissue[grid_row, grid_col * cols + c].astype(F32)
            live = jnp.where(same, flag, 0.0)
            q = q_s[c, :, lanes(i)] * 0.125
            qbd = jnp.concatenate([q] * SUB, axis=0) * same_low
            g = g_s[c, :, lanes(i)]
            gbd = jnp.concatenate([g] * SUB, axis=0) * live.astype(BF16)
            kc, vc = keys_of(0, c, i), keys_of(1, c, i)
            s = dot(kc, qbd, 1, 1) + bias[c]
            peak = jnp.max(s, axis=0, keepdims=True)
            p = jnp.exp(s - peak)
            w = p * (1.0 / jnp.sum(p, axis=0, keepdims=True))
            w_low = w.astype(BF16)
            att_t = (dot(vc, w_low, 0, 0) * live).astype(BF16)
            outs[0, c, :, lanes(i)] = fold_rows(att_t.T)
            out_dot = jnp.sum(att_t.astype(F32) * gbd.T.astype(F32), axis=0, keepdims=True)
            probe = dot(vc, gbd, 1, 1)
            ds = (w * (probe - out_dot)).astype(BF16)
            dq = jnp.where(same, dot(ds, kc, 0, 0), 0.0)
            outs[1, c, :, lanes(i)] = (fold_rows(dq) * 0.125).astype(BF16)
            for z, term in enumerate((dot(ds, qbd, 1, 0), dot(w_low, gbd, 1, 0))):
                drow[z, c : c + 3, :, lanes(i)] += term[: 3 * PIX].reshape(3, PIX, WIDTH)
                for v in range(nv):
                    first = 3 * (PIX + v * REACH)
                    dvert[z, v, c : c + 3, :, lanes(i)] += term[first : first + 3 * REACH].reshape(3, REACH, WIDTH)

    def merge(i):
        for d in range(2):
            beside(1 - d, lambda: vert_back(i, d).wait_recv())
        if seam is not None:
            @pl.when(seam)
            def _():
                relay_back(i, 0).wait_recv()
        for z in range(2):
            for v in range(nv):
                for c in range(cols):
                    vert_s[z, v, c, :, lanes(i)] = dvert[z, v, c + 1, :, lanes(i)].astype(BF16)
        for d, c in ((0, 0), (1, cols - 1)):
            def add(seamed, d=d, c=c):
                for z in range(2):
                    for v in range(nv):
                        edge_term = relay_r[z, :, lanes(i)] if seamed else hvert_r[d, z, v, :, lanes(i)]
                        vert_s[z, v, c, :, lanes(i)] = (
                            dvert[z, v, c + 1, :, lanes(i)] + edge_term.astype(F32)
                        ).astype(BF16)
            by_side(d, add)

    def send_down(i, terms=(0, 1)):
        for z in terms:
            for v in range(nv):
                down(i, z, v).start()

    def forward(i):
        for z in range(2):
            for v in range(nv):
                up(i, z, v).wait_recv()
        for d in range(2):
            def pass_on(seamed, d=d):
                for z in range(2):
                    (relay if seamed else edge)(i, z, d).start()
            by_side(d, pass_on)

    def step(i, _):
        forward(i)

        @pl.when(i + 1 < groups)
        def _():
            for z in range(2):
                for v in range(nv):
                    up(i + 1, z, v).start()

        @pl.when(i > 0)
        def _():
            merge(i - 1)
            if hasty is not None:
                pl.when(hasty)(lambda: send_down(i - 1))

        @pl.when(i == 0)
        def _():
            for copy in loads:
                copy.wait()
            for d in range(2):
                def wait(seamed, d=d):
                    for z in range(2):
                        sideways(z, d, seamed).wait_recv()
                by_side(1 - d, wait)

        for d in range(2):
            @functools.partial(beside, 1 - d)
            def _():
                for z in range(2):
                    edge(i, z, d).wait_recv()
        if seam is not None:
            for d in range(2):
                @pl.when(seams[1 - d])
                def _():
                    for z in range(2):
                        relay(i, z, d).wait_recv()
        attend(i, sorted({0, cols - 1}))
        for d, tile in ((0, 0), (1, cols + 1)):
            for z in range(2):
                hrow_s[d, z, :, lanes(i)] = drow[z, tile, :, lanes(i)].astype(BF16)
                for v in range(nv):
                    hvert_s[d, z, v, :, lanes(i)] = dvert[z, v, tile, :, lanes(i)].astype(BF16)
            def give(seamed, d=d):
                if seamed:
                    relay_back(i, d).start()
                row_back(i, d, seamed).start()
                vert_back(i, d).start()
            by_side(d, give)

        late = i > 0 if hasty is None else jnp.logical_and(i > 0, jnp.logical_not(hasty))
        pl.when(late)(lambda: send_down(i - 1))
        attend(i, range(1, cols - 1))
        for j in range(2):
            store(i, j).start()
        return 0

    lax.fori_loop(0, groups, step, 0)
    merge(groups - 1)
    send_down(groups - 1, (0,))
    if hasty is None:
        send_down(groups - 1, (1,))
    else:
        pl.when(hasty)(lambda: send_down(groups - 1, (1,)))

    def gather(i, _):
        for d, c in ((1, 0), (0, cols - 1)):
            def add(seamed, d=d, c=c):
                row_back(i, d, seamed).wait_recv()
                rows = pl.ds(rest, SKIP) if seamed else slice(None)
                for z in range(2):
                    drow[z, c + 1, rows, lanes(i)] += hrow_r[1 - d, z, rows, lanes(i)].astype(F32)
                    if seamed:
                        drow[z, c + 1, pl.ds(start[0], REACH), lanes(i)] += hvert_r[1 - d, z, 0, :, lanes(i)].astype(F32)
            by_side(1 - d, add)
        return 0

    def finish(i, _):
        for z in range(2):
            for v in range(nv):
                down(i, z, v).wait_recv()
            for c in range(cols):
                for v in range(nv):
                    drow[z, c + 1, pl.ds(start[v], REACH), lanes(i)] += vert_r[z, v, c, :, lanes(i)].astype(F32)
            outs[2 + z, :, :, lanes(i)] = drow[z, 1 : cols + 1, :, lanes(i)].astype(BF16)
            store(i, 2 + z).start()
        return 0

    lax.fori_loop(0, groups, gather, 0)
    lax.fori_loop(0, groups - 1, finish, 0)
    if hasty is not None:
        pl.when(jnp.logical_not(hasty))(lambda: send_down(groups - 1, (1,)))
    lax.fori_loop(groups - 1, groups, finish, 0)

    def drain(i, _):
        for z in range(2):
            for v in range(nv):
                up(i, z, v).wait_send()
            for d in range(2):
                beside(d, lambda: edge(i, z, d).wait_send())
        if seam is not None:
            for d in range(2):
                @pl.when(seams[d])
                def _():
                    for z in range(2):
                        relay(i, z, d).wait_send()
        for d in range(2):
            def sent(seamed, d=d):
                if seamed:
                    relay_back(i, d).wait_send()
                row_back(i, d, seamed).wait_send()
                vert_back(i, d).wait_send()
            by_side(d, sent)
        for z in range(2):
            for v in range(nv):
                down(i, z, v).wait_send()
        for j in range(4):
            store(i, j).wait()
        return 0

    for d in range(2):
        def sent(seamed, d=d):
            for z in range(2):
                sideways(z, d, seamed).wait_send()
        by_side(d, sent)
    lax.fori_loop(0, groups, drain, 0)


def copy_kernel(*refs):
    sem = refs[-1]
    copies = [pltpu.make_async_copy(refs[j], refs[4 + j], sem.at[j]) for j in range(4)]
    for copy in copies:
        copy.start()
    for copy in copies:
        copy.wait()


def local(query_states, key_states, value_states, grad_output, tissue_map):
    shape = query_states.shape
    cols, inner = shape[2], shape[4]
    q, k, v, g = (x.reshape(cols, PIX, inner) for x in (query_states, key_states, value_states, grad_output))
    count = lax.axis_size("row")
    nv = 1 if count // GRID_C == 2 else 2
    groups = inner // WIDTH
    seen = 3 * (PIX + nv * REACH)
    dma = pltpu.SemaphoreType.DMA
    anywhere = pl.BlockSpec(memory_space=pl.ANY)
    out = pl.pallas_call(
        functools.partial(kernel, count, nv, cols, groups),
        in_specs=[pl.BlockSpec(memory_space=pltpu.SMEM)] + [anywhere] * 4,
        out_specs=[anywhere] * 4,
        out_shape=[jax.ShapeDtypeStruct((cols, PIX, inner), BF16)] * 4,
        scratch_shapes=[
            pltpu.VMEM((cols, PIX, inner), BF16),
            pltpu.VMEM((cols, PIX, inner), BF16),
            pltpu.VMEM((2, cols + 2, PIX, inner), BF16),
            pltpu.VMEM((2, nv, cols + 2, REACH, inner), BF16),
            pltpu.VMEM((cols, seen, WIDTH), F32),
            pltpu.VMEM((2, cols + 2, PIX, inner), F32),
            pltpu.VMEM((2, nv, cols + 2, REACH, inner), F32),
            pltpu.VMEM((2, 2, PIX, inner), BF16),
            pltpu.VMEM((2, 2, nv, REACH, inner), BF16),
            pltpu.VMEM((2, 2, PIX, inner), BF16),
            pltpu.VMEM((2, 2, nv, REACH, inner), BF16),
            pltpu.VMEM((2, REACH, inner), BF16),
            pltpu.VMEM((2, nv, cols, REACH, inner), BF16),
            pltpu.VMEM((2, nv, cols, REACH, inner), BF16),
            pltpu.VMEM((4, cols, PIX, inner), BF16),
            dma((4,)), dma((groups, 4)),
            dma((2, 2)), dma((2, 2)),
            dma((groups, 2, nv)), dma((groups, 2, nv)),
            dma((groups, 2, 2)), dma((groups, 2, 2)),
            dma((groups, 2)), dma((groups, 2)),
            dma((groups, 2)), dma((groups, 2)),
            dma((groups, 2, nv)), dma((groups, 2, nv)),
            dma((groups, 2)), dma((groups, 2)), dma((groups,)), dma((groups,)),
        ],
        compiler_params=pltpu.CompilerParams(
            collective_id=0, has_side_effects=True, vmem_limit_bytes=40 << 20
        ),
        cost_estimate=pl.CostEstimate(
            flops=groups * cols * seen * WIDTH * WIDTH * 2 * 6,
            bytes_accessed=8 << 20,
            transcendentals=groups * cols * seen * WIDTH,
        ),
    )(*(pltpu.with_memory_space_constraint(x, pltpu.HBM) for x in (tissue_map, q, k, v, g)))
    out = pl.pallas_call(
        copy_kernel,
        in_specs=[anywhere] * 4,
        out_specs=[anywhere] * 4,
        out_shape=[jax.ShapeDtypeStruct((cols, PIX, inner), BF16)] * 4,
        scratch_shapes=[dma((4,))],
        compiler_params=pltpu.CompilerParams(vmem_limit_bytes=40 << 20),
    )(*out)
    return tuple(x.reshape(shape) for x in out)


def solution(mesh):
    blocks = P(("slide", "row"), None, None, None, None)
    return jax.shard_map(
        local,
        mesh=mesh,
        in_specs=(blocks, blocks, blocks, blocks, P("slide", None)),
        out_specs=(blocks, blocks, blocks, blocks),
        check_vma=False,
    )
```

```python
import functools

import jax
import jax.numpy as jnp
from jax import lax
from jax.experimental import pallas as pl
from jax.experimental.pallas import tpu as pltpu
from jax.sharding import PartitionSpec as P

HEAD_DIM = 64
TILE_SIDE = 8
WINDOW = 13
GRID_C = 8
PIX = TILE_SIDE * TILE_SIDE
HALF = (WINDOW - 1) // 2
REACH = HALF * TILE_SIDE
SKIP = PIX - REACH
WIDTH = 256
SUB = WIDTH // HEAD_DIM
MASKED = -1e30
F32 = jnp.float32
BF16 = jnp.bfloat16
MESH = pl.DeviceIdType.MESH


def dot(a, b, ca, cb):
    return lax.dot_general(a, b, (((ca,), (cb,)), ((), ())), preferred_element_type=F32)


def fold_rows(x):
    total = x[:PIX]
    for i in range(1, SUB):
        total = total + x[i * PIX : (i + 1) * PIX]
    return total


def kernel(
    count, nv, cols, groups,
    tissue, q_ref, k_ref, v_ref, g_ref, att_ref, dq_ref, dk_ref, dv_ref,
    q_s, g_s, rowx, vertx, bias, drow, dvert, hrow_s, hvert_s, hrow_r, hvert_r, relay_r, vert_s, vert_r, outs,
    load_sem, store_sem, side_ss, side_rs, up_ss, up_rs, edge_ss, edge_rs,
    hrow_ss, hrow_rs, hvert_ss, hvert_rs, vert_ss, vert_rs, relay_ss, relay_rs, relay_back_ss, relay_back_rs,
):
    slide, me = lax.axis_index("slide"), lax.axis_index("row")
    block = lax.rem(me + GRID_C // 2, count)
    grid_row, grid_col = lax.div(block, GRID_C), lax.rem(block, GRID_C)
    block_rows = count // GRID_C

    def at(distance):
        return (slide, lax.rem(me + distance + count, count))

    left, right = at(-1), at(1)
    if nv == 1:
        above = grid_row == 1
        hasty = above
        holds = jnp.logical_or(jnp.logical_not(above), lax.rem(grid_col, 2) == 1)
        distance = [GRID_C]
        start = [jnp.where(above, 0, SKIP)]
        places = [(jnp.where(above, -1, 1), jnp.where(above, -HALF, TILE_SIDE))]
        seam_left = grid_col == GRID_C // 2
        seam_right = grid_col == GRID_C // 2 - 1
        seam = jnp.logical_or(seam_left, seam_right)
        across = at(jnp.where(seam_left, GRID_C - 1, GRID_C + 1))
    else:
        distance = [GRID_C, -GRID_C]
        start = [jnp.int32(SKIP), jnp.int32(0)]
        places = [(-1, -HALF), (1, TILE_SIDE)]
        seam_left = seam_right = seam = hasty = None
    start = [pl.multiple_of(x, 16) for x in start]
    seams = (seam_left, seam_right)
    walls = (grid_col == 0, grid_col == GRID_C - 1)
    if seam is not None:
        start_other = pl.multiple_of(SKIP - start[0], 16)
        rest = pl.multiple_of(jnp.where(above, REACH, 0), 16)

    def lanes(i):
        return pl.ds(pl.multiple_of(i * WIDTH, WIDTH), WIDTH)

    kv = (k_ref, v_ref)
    loads = [pltpu.make_async_copy(x, y, load_sem.at[j]) for j, (x, y) in enumerate((
        (k_ref, rowx.at[0, pl.ds(1, cols)]), (v_ref, rowx.at[1, pl.ds(1, cols)]), (q_ref, q_s), (g_ref, g_s),
    ))]

    def remote(src, dst, ss, rs, device):
        return pltpu.make_async_remote_copy(
            src_ref=src, dst_ref=dst, send_sem=ss, recv_sem=rs, device_id=device, device_id_type=MESH
        )

    def up(i, z, v):
        return remote(
            kv[z].at[:, pl.ds(start[v], REACH), lanes(i)],
            vertx.at[z, v, pl.ds(1, cols), :, lanes(i)],
            up_ss.at[i, z, v], up_rs.at[i, z, v], at(distance[v]),
        )

    def sideways(z, d, seamed=False):
        src, dst = kv[z].at[0 if d == 0 else cols - 1], rowx.at[z, cols + 1 if d == 0 else 0]
        if seamed:
            src, dst = src.at[pl.ds(rest, SKIP)], dst.at[pl.ds(rest, SKIP)]
        return remote(src, dst, side_ss.at[z, d], side_rs.at[z, d], left if d == 0 else right)

    def relay(i, z, d):
        return remote(
            vertx.at[z, 0, 1 if d == 0 else cols, :, lanes(i)],
            rowx.at[z, cols + 1 if d == 0 else 0, pl.ds(start_other, REACH), lanes(i)],
            relay_ss.at[i, z], relay_rs.at[i, z], across,
        )

    def by_side(d, run):
        if seam is None:
            pl.when(jnp.logical_not(walls[d]))(lambda: run(False))
        else:
            pl.when(seams[d])(lambda: run(True))
            pl.when(jnp.logical_not(jnp.logical_or(seams[d], walls[d])))(lambda: run(False))

    def beside(d, run):
        pl.when(jnp.logical_not(walls[d]))(run)

    def edge(i, z, d):
        return remote(
            vertx.at[z, :, 1 if d == 0 else cols, :, lanes(i)], vertx.at[z, :, cols + 1 if d == 0 else 0, :, lanes(i)],
            edge_ss.at[i, z, d], edge_rs.at[i, z, d], left if d == 0 else right,
        )

    def diagonal(i, z, d):
        return remote(
            kv[z].at[0 if d == 0 else cols - 1, pl.ds(start[0], REACH), lanes(i)],
            vertx.at[z, 0, cols + 1 if d == 0 else 0, :, lanes(i)],
            edge_ss.at[i, z, d], edge_rs.at[i, z, d], across,
        )

    def row_back(i, d, seamed=False):
        rows = pl.ds(rest, SKIP) if seamed else slice(None)
        return remote(
            hrow_s.at[d, :, rows, lanes(i)], hrow_r.at[1 - d, :, rows, lanes(i)],
            hrow_ss.at[i, d], hrow_rs.at[i, d], left if d == 0 else right,
        )

    def relay_back(i, d):
        return remote(
            hrow_s.at[d, :, pl.ds(start[0], REACH), lanes(i)], relay_r.at[:, :, lanes(i)],
            relay_back_ss.at[i], relay_back_rs.at[i], across,
        )

    def vert_back(i, d):
        device = left if d == 0 else right
        if seam is not None:
            device = (slide, jnp.where(seams[d], across[1], device[1]))
        return remote(
            hvert_s.at[d, :, :, :, lanes(i)], hvert_r.at[1 - d, :, :, :, lanes(i)],
            hvert_ss.at[i, d], hvert_rs.at[i, d], device,
        )

    def down(i, z, v):
        return remote(
            vert_s.at[z, v, :, :, lanes(i)], vert_r.at[z, v, :, :, lanes(i)],
            vert_ss.at[i, z, v], vert_rs.at[i, z, v], at(-distance[v]),
        )

    def store(i, j):
        return pltpu.make_async_copy(
            outs.at[j, :, :, lanes(i)], (att_ref, dq_ref, dk_ref, dv_ref)[j].at[:, :, lanes(i)], store_sem.at[i, j]
        )

    barrier = pltpu.get_barrier_semaphore()
    def greet(device):
        pl.semaphore_signal(barrier, inc=1, device_id=device, device_id_type=MESH)
    for x in distance:
        greet(at(x))
    if seam is not None:
        pl.when(seam)(lambda: greet(across))
    for d in range(2):
        beside(d, lambda: greet((left, right)[d]))
    for copy in loads:
        copy.start()
    peers = 2 + nv - jnp.logical_or(*walls).astype(jnp.int32)
    if seam is not None:
        peers = peers + seam.astype(jnp.int32)
    pl.semaphore_wait(barrier, peers)

    for z in range(2):
        for v in range(nv):
            up(0, z, v).start()
    for d in range(2):
        def send(seamed, d=d):
            for z in range(2):
                sideways(z, d, seamed).start()
        by_side(d, send)
    if seam is not None:
        for d in range(2):
            @pl.when(seams[d])
            def _():
                for i in range(groups):
                    for z in range(2):
                        diagonal(i, z, d).start()

    query = lax.broadcasted_iota(jnp.int32, (PIX, WIDTH), 1) % PIX
    line = lax.broadcasted_iota(jnp.int32, (PIX, WIDTH), 0)
    top = 0
    for step_row, first, rows in [(0, 0, PIX)] + [(r, f, REACH) for r, f in places]:
        row_gap = first + line[:rows] // TILE_SIDE - query[:rows] // TILE_SIDE
        row = grid_row + step_row
        for step in (-1, 0, 1):
            col_gap = TILE_SIDE * step + line[:rows] % TILE_SIDE - query[:rows] % TILE_SIDE
            near = (jnp.abs(row_gap) <= HALF) & (jnp.abs(col_gap) <= HALF)
            near = jnp.where(near, 0.0, MASKED)
            for c in range(cols):
                col = grid_col * cols + c + step
                inside = (row >= 0) & (row < block_rows) & (col >= 0) & (col < GRID_C * cols)
                flag = tissue[jnp.clip(row, 0, block_rows - 1), jnp.clip(col, 0, GRID_C * cols - 1)]
                shut = jnp.where(inside & (flag > 0), 0.0, MASKED)
                bias[c, top : top + rows] = jnp.minimum(near, shut)
            top += rows
    for d, tile in ((0, 0), (1, cols + 1)):
        @pl.when(walls[d])
        def _():
            rowx[:, tile] = jnp.zeros((2, PIX, rowx.shape[-1]), BF16)
            vertx[:, :, tile] = jnp.zeros((2, nv, REACH, rowx.shape[-1]), BF16)
    drow[...] = jnp.zeros_like(drow)
    dvert[...] = jnp.zeros_like(dvert)

    same = (
        lax.broadcasted_iota(jnp.int32, (WIDTH, WIDTH), 0) // PIX
        == lax.broadcasted_iota(jnp.int32, (WIDTH, WIDTH), 1) // HEAD_DIM
    )
    same_low = jnp.where(same, 1.0, 0.0).astype(BF16)

    def keys_of(z, c, i):
        parts = [rowx[z, c : c + 3, :, lanes(i)].reshape(3 * PIX, WIDTH)]
        for v in range(nv):
            parts.append(vertx[z, v, c : c + 3, :, lanes(i)].reshape(3 * REACH, WIDTH))
        return jnp.concatenate(parts, axis=0)

    def attend(i, columns):
        for c in columns:
            flag = tissue[grid_row, grid_col * cols + c].astype(F32)
            live = jnp.where(same, flag, 0.0)
            q = q_s[c, :, lanes(i)] * 0.125
            qbd = jnp.concatenate([q] * SUB, axis=0) * same_low
            g = g_s[c, :, lanes(i)]
            gbd = jnp.concatenate([g] * SUB, axis=0) * live.astype(BF16)
            kc, vc = keys_of(0, c, i), keys_of(1, c, i)
            s = dot(kc, qbd, 1, 1) + bias[c]
            peak = jnp.max(s, axis=0, keepdims=True)
            p = jnp.exp(s - peak)
            w = p * (1.0 / jnp.sum(p, axis=0, keepdims=True))
            w_low = w.astype(BF16)
            att_t = (dot(vc, w_low, 0, 0) * live).astype(BF16)
            outs[0, c, :, lanes(i)] = fold_rows(att_t.T)
            out_dot = jnp.sum(att_t.astype(F32) * gbd.T.astype(F32), axis=0, keepdims=True)
            probe = dot(vc, gbd, 1, 1)
            ds = (w * (probe - out_dot)).astype(BF16)
            dq = jnp.where(same, dot(ds, kc, 0, 0), 0.0)
            outs[1, c, :, lanes(i)] = (fold_rows(dq) * 0.125).astype(BF16)
            for z, term in enumerate((dot(ds, qbd, 1, 0), dot(w_low, gbd, 1, 0))):
                drow[z, c : c + 3, :, lanes(i)] += term[: 3 * PIX].reshape(3, PIX, WIDTH)
                for v in range(nv):
                    first = 3 * (PIX + v * REACH)
                    dvert[z, v, c : c + 3, :, lanes(i)] += term[first : first + 3 * REACH].reshape(3, REACH, WIDTH)

    def merge(i):
        for d in range(2):
            beside(1 - d, lambda: vert_back(i, d).wait_recv())
        if seam is not None:
            @pl.when(seam)
            def _():
                relay_back(i, 0).wait_recv()
        for z in range(2):
            for v in range(nv):
                for c in range(cols):
                    vert_s[z, v, c, :, lanes(i)] = dvert[z, v, c + 1, :, lanes(i)].astype(BF16)
        for d, c in ((0, 0), (1, cols - 1)):
            def add(seamed, d=d, c=c):
                for z in range(2):
                    for v in range(nv):
                        edge_term = relay_r[z, :, lanes(i)] if seamed else hvert_r[d, z, v, :, lanes(i)]
                        vert_s[z, v, c, :, lanes(i)] = (
                            dvert[z, v, c + 1, :, lanes(i)] + edge_term.astype(F32)
                        ).astype(BF16)
            by_side(d, add)

    def send_down(i, terms=(0, 1)):
        for z in terms:
            for v in range(nv):
                down(i, z, v).start()

    def forward(i):
        for z in range(2):
            for v in range(nv):
                up(i, z, v).wait_recv()
        for d in range(2):
            def pass_on(seamed, d=d):
                for z in range(2):
                    (relay if seamed else edge)(i, z, d).start()
            by_side(d, pass_on)

    def step(i, _):
        forward(i)

        @pl.when(i + 1 < groups)
        def _():
            for z in range(2):
                for v in range(nv):
                    up(i + 1, z, v).start()

        @pl.when(i > 0)
        def _():
            merge(i - 1)
            if hasty is not None:
                pl.when(hasty)(lambda: send_down(i - 1))

        @pl.when(i == 0)
        def _():
            for copy in loads:
                copy.wait()
            for d in range(2):
                def wait(seamed, d=d):
                    for z in range(2):
                        sideways(z, d, seamed).wait_recv()
                by_side(1 - d, wait)

        for d in range(2):
            @functools.partial(beside, 1 - d)
            def _():
                for z in range(2):
                    edge(i, z, d).wait_recv()
        if seam is not None:
            for d in range(2):
                @pl.when(seams[1 - d])
                def _():
                    for z in range(2):
                        relay(i, z, d).wait_recv()
        attend(i, sorted({0, cols - 1}))
        for d, tile in ((0, 0), (1, cols + 1)):
            for z in range(2):
                hrow_s[d, z, :, lanes(i)] = drow[z, tile, :, lanes(i)].astype(BF16)
                for v in range(nv):
                    hvert_s[d, z, v, :, lanes(i)] = dvert[z, v, tile, :, lanes(i)].astype(BF16)
            def give(seamed, d=d):
                if seamed:
                    relay_back(i, d).start()
                row_back(i, d, seamed).start()
                vert_back(i, d).start()
            by_side(d, give)

        late = i > 0 if hasty is None else jnp.logical_and(i > 0, jnp.logical_not(hasty))
        pl.when(late)(lambda: send_down(i - 1))
        attend(i, range(1, cols - 1))
        for j in range(2):
            store(i, j).start()
        return 0

    lax.fori_loop(0, groups, step, 0)
    merge(groups - 1)
    send_down(groups - 1, (0,))
    if hasty is None:
        send_down(groups - 1, (1,))
    else:
        pl.when(jnp.logical_not(holds))(lambda: send_down(groups - 1, (1,)))

    def gather(i, _):
        for d, c in ((1, 0), (0, cols - 1)):
            def add(seamed, d=d, c=c):
                row_back(i, d, seamed).wait_recv()
                rows = pl.ds(rest, SKIP) if seamed else slice(None)
                for z in range(2):
                    drow[z, c + 1, rows, lanes(i)] += hrow_r[1 - d, z, rows, lanes(i)].astype(F32)
                    if seamed:
                        drow[z, c + 1, pl.ds(start[0], REACH), lanes(i)] += hvert_r[1 - d, z, 0, :, lanes(i)].astype(F32)
            by_side(1 - d, add)
        return 0

    def finish(i, _):
        for z in range(2):
            for v in range(nv):
                down(i, z, v).wait_recv()
            for c in range(cols):
                for v in range(nv):
                    drow[z, c + 1, pl.ds(start[v], REACH), lanes(i)] += vert_r[z, v, c, :, lanes(i)].astype(F32)
            outs[2 + z, :, :, lanes(i)] = drow[z, 1 : cols + 1, :, lanes(i)].astype(BF16)
            store(i, 2 + z).start()
        return 0

    lax.fori_loop(0, groups, gather, 0)
    lax.fori_loop(0, groups - 1, finish, 0)
    if hasty is not None:
        pl.when(holds)(lambda: send_down(groups - 1, (1,)))
    lax.fori_loop(groups - 1, groups, finish, 0)

    def drain(i, _):
        for z in range(2):
            for v in range(nv):
                up(i, z, v).wait_send()
            for d in range(2):
                beside(d, lambda: edge(i, z, d).wait_send())
        if seam is not None:
            for d in range(2):
                @pl.when(seams[d])
                def _():
                    for z in range(2):
                        relay(i, z, d).wait_send()
        for d in range(2):
            def sent(seamed, d=d):
                if seamed:
                    relay_back(i, d).wait_send()
                row_back(i, d, seamed).wait_send()
                vert_back(i, d).wait_send()
            by_side(d, sent)
        for z in range(2):
            for v in range(nv):
                down(i, z, v).wait_send()
        for j in range(4):
            store(i, j).wait()
        return 0

    for d in range(2):
        def sent(seamed, d=d):
            for z in range(2):
                sideways(z, d, seamed).wait_send()
        by_side(d, sent)
    lax.fori_loop(0, groups, drain, 0)


def copy_kernel(*refs):
    sem = refs[-1]
    copies = [pltpu.make_async_copy(refs[j], refs[4 + j], sem.at[j]) for j in range(4)]
    for copy in copies:
        copy.start()
    for copy in copies:
        copy.wait()


def local(query_states, key_states, value_states, grad_output, tissue_map):
    shape = query_states.shape
    cols, inner = shape[2], shape[4]
    q, k, v, g = (x.reshape(cols, PIX, inner) for x in (query_states, key_states, value_states, grad_output))
    count = lax.axis_size("row")
    nv = 1 if count // GRID_C == 2 else 2
    groups = inner // WIDTH
    seen = 3 * (PIX + nv * REACH)
    dma = pltpu.SemaphoreType.DMA
    anywhere = pl.BlockSpec(memory_space=pl.ANY)
    out = pl.pallas_call(
        functools.partial(kernel, count, nv, cols, groups),
        in_specs=[pl.BlockSpec(memory_space=pltpu.SMEM)] + [anywhere] * 4,
        out_specs=[anywhere] * 4,
        out_shape=[jax.ShapeDtypeStruct((cols, PIX, inner), BF16)] * 4,
        scratch_shapes=[
            pltpu.VMEM((cols, PIX, inner), BF16),
            pltpu.VMEM((cols, PIX, inner), BF16),
            pltpu.VMEM((2, cols + 2, PIX, inner), BF16),
            pltpu.VMEM((2, nv, cols + 2, REACH, inner), BF16),
            pltpu.VMEM((cols, seen, WIDTH), F32),
            pltpu.VMEM((2, cols + 2, PIX, inner), F32),
            pltpu.VMEM((2, nv, cols + 2, REACH, inner), F32),
            pltpu.VMEM((2, 2, PIX, inner), BF16),
            pltpu.VMEM((2, 2, nv, REACH, inner), BF16),
            pltpu.VMEM((2, 2, PIX, inner), BF16),
            pltpu.VMEM((2, 2, nv, REACH, inner), BF16),
            pltpu.VMEM((2, REACH, inner), BF16),
            pltpu.VMEM((2, nv, cols, REACH, inner), BF16),
            pltpu.VMEM((2, nv, cols, REACH, inner), BF16),
            pltpu.VMEM((4, cols, PIX, inner), BF16),
            dma((4,)), dma((groups, 4)),
            dma((2, 2)), dma((2, 2)),
            dma((groups, 2, nv)), dma((groups, 2, nv)),
            dma((groups, 2, 2)), dma((groups, 2, 2)),
            dma((groups, 2)), dma((groups, 2)),
            dma((groups, 2)), dma((groups, 2)),
            dma((groups, 2, nv)), dma((groups, 2, nv)),
            dma((groups, 2)), dma((groups, 2)), dma((groups,)), dma((groups,)),
        ],
        compiler_params=pltpu.CompilerParams(
            collective_id=0, has_side_effects=True, vmem_limit_bytes=40 << 20
        ),
        cost_estimate=pl.CostEstimate(
            flops=groups * cols * seen * WIDTH * WIDTH * 2 * 6,
            bytes_accessed=8 << 20,
            transcendentals=groups * cols * seen * WIDTH,
        ),
    )(*(pltpu.with_memory_space_constraint(x, pltpu.HBM) for x in (tissue_map, q, k, v, g)))
    out = pl.pallas_call(
        copy_kernel,
        in_specs=[anywhere] * 4,
        out_specs=[anywhere] * 4,
        out_shape=[jax.ShapeDtypeStruct((cols, PIX, inner), BF16)] * 4,
        scratch_shapes=[dma((4,))],
        compiler_params=pltpu.CompilerParams(vmem_limit_bytes=40 << 20),
    )(*out)
    return tuple(x.reshape(shape) for x in out)


def solution(mesh):
    blocks = P(("slide", "row"), None, None, None, None)
    return jax.shard_map(
        local,
        mesh=mesh,
        in_specs=(blocks, blocks, blocks, blocks, P("slide", None)),
        out_specs=(blocks, blocks, blocks, blocks),
        check_vma=False,
    )
```
